32 devices in a mesh: dom: 4 (over z), shard: 8 (over y, x, core).
Axes of the slice: x: 2, y: 2, z: 4, core: 2. Of those that a mesh axis runs over, the one named last changes fastest.
Arguments:
- features: bfloat16 [131072, 1024], P(('dom', 'shard')), may hold values from -6 to 6
- enc_weight: bfloat16 [1024, 512], replicated, may hold values from -0.1875 to 0.1875
- pack_index: int32 [4, 8, 8, 512], P('dom', 'shard'), may hold values from 0 to 4095, as said below
- place_index: int32 [4, 8, 4096], P('dom', 'shard'), may hold values from 0 to 4095, as said below
- halo_send_one: int32 [4, 8, 4, 8, 16], P('dom', 'shard'), may hold values from 0 to 4096, as said below
- halo_send_two: int32 [4, 8, 4, 8, 16], P('dom', 'shard'), may hold values from 0 to 4096, as said below
- tile_index_one: int32 [1024, 6], P(('dom', 'shard')), may hold values from 0 to 35
- tile_index_two: int32 [1024, 6], P(('dom', 'shard')), may hold values from 0 to 35
- tile_live_one: int32 [1024], P(('dom', 'shard')), may hold values from 1 to 6, as said below
- tile_live_two: int32 [1024], P(('dom', 'shard')), may hold values from 1 to 6, as said below
- tiles_one: bfloat16 [1024, 6, 128, 128], P(('dom', 'shard')), may hold values from 0 to 2, as said below
- tiles_two: bfloat16 [1024, 6, 128, 128], P(('dom', 'shard')), may hold values from 0 to 2, as said below
- degree: int32 [131072], P(('dom', 'shard')), may hold values from 32 to 255
- self_weight_one: bfloat16 [512, 512], replicated, may hold values from -0.25 to 0.25
- neigh_weight_one: bfloat16 [512, 512], replicated, may hold values from -0.25 to 0.25
- self_weight_two: bfloat16 [512, 512], replicated, may hold values from -0.25 to 0.25
- neigh_weight_two: bfloat16 [512, 512], replicated, may hold values from -0.25 to 0.25
- head_weight: bfloat16 [512], replicated, may hold values from -0.25 to 0.25
Outputs:
- embedding: bfloat16 [131072, 512], P(('dom', 'shard'))
- probability: float32 [131072], P(('dom', 'shard'))
The draws below stay inside these ranges and needn't reach their ends.
Inputs may be any that keep to these rules, and one draw needn't show every extreme that they name: pack_index[d, s, t, :] lists the 512 hash-order rows that device s of group d sends to owner t; every local row is sent exactly once. place_index[d, t, :] is a permutation of the slots that owner t receives. halo_send_one[d, s, d2, s2, :] lists rows of device (d, s) for device (d2, s2), then 4096 in empty slots; a device sends nothing to itself, exactly 16 rows to one device and 1 to 16 rows to every other. `halo_send_two`: as halo_send_one. `tile_live_one`: every device has a block with all 6 slots live. `tile_live_two`: every device has a block with all 6 slots live. `tiles_one`: nonnegative edge weights. `tiles_two`: nonnegative edge weights.
All inputs are finite; a program needn't handle non-finite values.
Results may differ from the reference program's by a relative error of at most 0.0054.
Values may be sent and summed in bfloat16 or wider, within the bound.
A program may use at most 192 MiB of HBM per device.

```python
import jax
import jax.numpy as jnp
from jax import lax

IN_WIDTH = 1024
WIDTH = 512
ROWS_DEV = 4096
TILE_SIZE = 128
TILE_SLOTS = 6
BOUNDARY_CAP = 16
GROUPS = 4
GROUP_SIZE = 8
DEVICE_COUNT = 32
TARGETS = 131072
BLOCKS_DEV = 32
BLOCKS_ALL = 1024
SOURCE_BLOCKS = 36
RELAY_CAP = 512
N_DOM = 4
N_SHARD = 8


def relay_tables(key):

    def one_group(group_key):
        key_order, key_place = jax.random.split(group_key)
        orders = jax.vmap(lambda kk: jax.random.permutation(kk, ROWS_DEV))(jax.random.split(key_order, GROUP_SIZE))
        packing = orders.reshape(GROUP_SIZE, GROUP_SIZE, RELAY_CAP).astype(jnp.int32)
        placing = jax.vmap(lambda kk: jax.random.permutation(kk, ROWS_DEV))(jax.random.split(key_place, GROUP_SIZE)).astype(jnp.int32)
        return (packing, placing)
    return jax.vmap(one_group)(jax.random.split(jax.random.fold_in(key, 11), GROUPS))


def draw_pack_index(key, part):
    return relay_tables(key)[0]


def draw_place_index(key, part):
    return relay_tables(key)[1]


def halo_table(key):
    key_count, key_rows = jax.random.split(key)
    counts = jax.random.randint(key_count, (DEVICE_COUNT, DEVICE_COUNT), 1, BOUNDARY_CAP + 1)
    source = jnp.arange(DEVICE_COUNT)[:, None]
    target = jnp.arange(DEVICE_COUNT)[None, :]
    counts = jnp.where(target == (source + DEVICE_COUNT // 2 + 1) % DEVICE_COUNT, BOUNDARY_CAP, counts)
    counts = jnp.where(target == source, 0, counts)
    picks = jax.random.randint(key_rows, (DEVICE_COUNT, DEVICE_COUNT, BOUNDARY_CAP), 0, ROWS_DEV)
    slots = jnp.arange(BOUNDARY_CAP)
    table = jnp.where(slots[None, None, :] < counts[:, :, None], picks, ROWS_DEV)
    return table.reshape(GROUPS, GROUP_SIZE, GROUPS, GROUP_SIZE, BOUNDARY_CAP).astype(jnp.int32)


def draw_halo_send_one(key, part):
    return halo_table(jax.random.fold_in(key, 21))


def draw_halo_send_two(key, part):
    return halo_table(jax.random.fold_in(key, 22))


def live_table(key):
    key_count, key_full = jax.random.split(key)
    counts = jax.random.randint(key_count, (DEVICE_COUNT, BLOCKS_DEV), 1, TILE_SLOTS + 1)
    full = jax.random.randint(key_full, (DEVICE_COUNT,), 0, BLOCKS_DEV)
    counts = jnp.where(jnp.arange(BLOCKS_DEV)[None, :] == full[:, None], TILE_SLOTS, counts)
    return counts.reshape(BLOCKS_ALL).astype(jnp.int32)


def draw_tile_live_one(key, part):
    return live_table(jax.random.fold_in(key, 31))


def draw_tile_live_two(key, part):
    return live_table(jax.random.fold_in(key, 32))


def tile_table(key):
    key_mask, key_value = jax.random.split(key)
    shape = (BLOCKS_ALL, TILE_SLOTS, TILE_SIZE, TILE_SIZE)
    present = jax.random.bernoulli(key_mask, 0.5, shape).astype(jnp.float32)
    value = jax.random.uniform(key_value, shape, jnp.float32, 0.5, 1.5)
    return (present * value).astype(jnp.bfloat16)


def draw_tiles_one(key, part):
    return tile_table(jax.random.fold_in(key, 41))


def draw_tiles_two(key, part):
    return tile_table(jax.random.fold_in(key, 42))


def plant(array, rng, least, largest):
    longest = array.shape.index(max(array.shape))
    spots = []
    for shift in (0, 1):
        where = [jax.random.randint(jax.random.fold_in(rng, axis), (), 0, length) for axis, length in enumerate(array.shape)]
        where[longest] = (where[longest] + shift) % array.shape[longest]
        spots.append(tuple(where))
    return array.at[spots[0]].set(least).at[spots[1]].set(largest)


def levels(rng, extent, pieces, low, largest):
    gain, own = 1.0, jax.random.fold_in(rng, 6)
    for position, parts in pieces:
        heights = jnp.exp(jax.random.uniform(jax.random.fold_in(own, position), (parts,), jnp.float32, low / len(pieces), largest / len(pieces)))
        gain = gain * jnp.repeat(heights, extent[position] // parts).reshape([-1 if axis == position else 1 for axis in range(len(extent))])
    return gain


def centred(own_key, shape, deviation, reach, cuts=(), kind=jnp.bfloat16):
    entries = deviation * jax.random.normal(own_key, shape, jnp.float32)
    if cuts:
        entries = entries * levels(own_key, shape, cuts, -0.22, 0.18)
    return jnp.clip(entries, -reach, reach).astype(kind)


def setup_inputs(seed: int = 0) -> dict:
    streams_of = jax.random.split(jax.random.key(seed), 19)
    features = centred(streams_of[0], (TARGETS, IN_WIDTH), 1.0, 6.0, ((0, 32),))
    enc_weight = centred(streams_of[1], (IN_WIDTH, WIDTH), IN_WIDTH ** -0.5, 0.1875)
    pack_index = draw_pack_index(jax.random.fold_in(streams_of[18], 71), 0)
    place_index = draw_place_index(jax.random.fold_in(streams_of[18], 71), 0)
    halo_send_one = draw_halo_send_one(jax.random.fold_in(streams_of[18], 71), 0)
    halo_send_two = draw_halo_send_two(jax.random.fold_in(streams_of[18], 71), 0)
    tile_index_one = plant(jax.random.randint(streams_of[6], (BLOCKS_ALL, TILE_SLOTS), 0, SOURCE_BLOCKS), jax.random.fold_in(streams_of[6], 1), 0, SOURCE_BLOCKS - 1).astype(jnp.int32)
    tile_index_two = plant(jax.random.randint(streams_of[7], (BLOCKS_ALL, TILE_SLOTS), 0, SOURCE_BLOCKS), jax.random.fold_in(streams_of[7], 1), 0, SOURCE_BLOCKS - 1).astype(jnp.int32)
    tile_live_one = draw_tile_live_one(jax.random.fold_in(streams_of[18], 71), 0)
    tile_live_two = draw_tile_live_two(jax.random.fold_in(streams_of[18], 71), 0)
    tiles_one = draw_tiles_one(jax.random.fold_in(streams_of[18], 71), 0)
    tiles_two = draw_tiles_two(jax.random.fold_in(streams_of[18], 71), 0)
    degree = plant(jax.random.randint(streams_of[12], (TARGETS,), 32, 256), jax.random.fold_in(streams_of[12], 1), 32, 255).astype(jnp.int32)
    self_weight_one = centred(streams_of[13], (WIDTH, WIDTH), WIDTH ** -0.5, 0.25)
    neigh_weight_one = centred(streams_of[14], (WIDTH, WIDTH), WIDTH ** -0.5, 0.25)
    self_weight_two = centred(streams_of[15], (WIDTH, WIDTH), WIDTH ** -0.5, 0.25)
    neigh_weight_two = centred(streams_of[16], (WIDTH, WIDTH), WIDTH ** -0.5, 0.25)
    head_weight = centred(streams_of[17], (WIDTH,), WIDTH ** -0.5, 0.25)
    return {"features": features, "enc_weight": enc_weight, "pack_index": pack_index, "place_index": place_index, "halo_send_one": halo_send_one, "halo_send_two": halo_send_two, "tile_index_one": tile_index_one, "tile_index_two": tile_index_two, "tile_live_one": tile_live_one, "tile_live_two": tile_live_two, "tiles_one": tiles_one, "tiles_two": tiles_two, "degree": degree, "self_weight_one": self_weight_one, "neigh_weight_one": neigh_weight_one, "self_weight_two": self_weight_two, "neigh_weight_two": neigh_weight_two, "head_weight": head_weight}


def sage_layer(hidden_in, halo_send, tile_index, tile_live, tiles, degree, self_weight, neigh_weight):
    count = N_DOM * N_SHARD
    width = hidden_in.shape[-1]
    padded = jnp.concatenate([hidden_in, jnp.zeros((count, 1, width), jnp.bfloat16)], axis=1)
    sendlist = halo_send.reshape(count, count, BOUNDARY_CAP)

    def per_device(packed):
        device, own_rows, index_dev, live_dev, tiles_dev, degree_dev = packed
        columns = lax.dynamic_index_in_dim(sendlist, device, axis=1, keepdims=False)
        boundary = jax.vmap(lambda table, picks: table[picks])(padded, columns).reshape(count * BOUNDARY_CAP, width)
        sources = jnp.concatenate([own_rows, boundary], axis=0).reshape(-1, TILE_SIZE, width)
        slot_live = jnp.arange(TILE_SLOTS, dtype=jnp.int32)[None, :] < live_dev[:, None]
        masked = jnp.where(slot_live[:, :, None, None], tiles_dev, jnp.zeros((), jnp.bfloat16))
        picked = sources[index_dev]
        summed = jnp.einsum('bkij,bkjf->bif', masked.astype(jnp.float32), picked.astype(jnp.float32)).reshape(ROWS_DEV, width)
        aggregate = (summed / degree_dev[:, None].astype(jnp.float32)).astype(jnp.bfloat16)
        mixed = jnp.dot(own_rows, self_weight, preferred_element_type=jnp.float32) + jnp.dot(aggregate, neigh_weight, preferred_element_type=jnp.float32)
        active = jnp.maximum(mixed, 0.0)
        scaled = active * lax.rsqrt(lax.optimization_barrier(jnp.mean(active * active, axis=-1, keepdims=True)) + 1e-06)
        return scaled.astype(jnp.bfloat16)
    return lax.map(per_device, (jnp.arange(count, dtype=jnp.int32), hidden_in, tile_index.reshape(count, BLOCKS_DEV, TILE_SLOTS), tile_live.reshape(count, BLOCKS_DEV), tiles.reshape(count, BLOCKS_DEV, TILE_SLOTS, TILE_SIZE, TILE_SIZE), degree.reshape(count, ROWS_DEV)))

def reference(features, enc_weight, pack_index, place_index, halo_send_one, halo_send_two, tile_index_one, tile_index_two, tile_live_one, tile_live_two, tiles_one, tiles_two, degree, self_weight_one, neigh_weight_one, self_weight_two, neigh_weight_two, head_weight):
    count = N_DOM * N_SHARD
    encoded = jnp.maximum(jnp.dot(features, enc_weight, preferred_element_type=jnp.float32), 0.0).astype(jnp.bfloat16)
    width = encoded.shape[1]
    hashed = encoded.reshape(N_DOM, N_SHARD, ROWS_DEV, width)

    def relay_group(packed):
        block, packing, placing = packed
        outgoing = jax.vmap(lambda table, picks: table[picks.reshape(-1)].reshape(N_SHARD, RELAY_CAP, width))(block, packing)
        arrived = jnp.transpose(outgoing, (1, 0, 2, 3)).reshape(N_SHARD, N_SHARD * RELAY_CAP, width)
        return jax.vmap(lambda table, picks: table[picks])(arrived, placing)
    owned = lax.map(relay_group, (hashed, pack_index, place_index)).reshape(count, ROWS_DEV, width)
    layer_one = sage_layer(owned, halo_send_one, tile_index_one, tile_live_one, tiles_one, degree, self_weight_one, neigh_weight_one)
    layer_two = sage_layer(layer_one, halo_send_two, tile_index_two, tile_live_two, tiles_two, degree, self_weight_two, neigh_weight_two)
    embedding = layer_two.reshape(count * ROWS_DEV, width)
    probability = jax.nn.sigmoid(jnp.dot(embedding, head_weight, preferred_element_type=jnp.float32))
    return (embedding, probability)
```

```python
import functools

import jax
import jax.numpy as jnp
from jax import lax
from jax.experimental import pallas as pl
from jax.experimental.pallas import tpu as pltpu
from jax.sharding import PartitionSpec as P

LANES = 128
STEP = 512
RING = 4
UNROLL = 32
ABREAST = 3
AHEAD = 2
VMEM_LIMIT = 60 << 20
MESH = pl.DeviceIdType.MESH
NOWHERE = -(1 << 20)


def dot(a, b):
    return jnp.dot(a, b, preferred_element_type=jnp.float32)


def span(first, count):
    return pl.ds(pl.multiple_of(first, count), count)


def flipped(a, b, n):
    total, bit = 0, 1
    while bit < n:
        p, q = (a // bit) % 2, (b // bit) % 2
        total = total + bit * (p + q - 2 * p * q)
        bit *= 2
    return total


def turned(step, n):
    half = n // 2
    return jnp.where(step < half, 2 * step, (2 * (step - half) + 3) % n)


def kernel(
    groups,
    n,
    features,
    enc_weight,
    packing,
    placing,
    placing_row,
    sending_one,
    sending_two,
    index_one,
    index_two,
    live_one,
    live_two,
    tiles_one,
    tiles_two,
    degree,
    self_one,
    neigh_one,
    self_two,
    neigh_two,
    head,
    embedding,
    probability,
    feats,
    weight,
    weights,
    tiles,
    work,
    picked,
    stage,
    recv,
    owned,
    place_ids,
    edge_ids,
    share,
    edge,
    halo,
    halo_mixed,
    feat_sem,
    load_sem,
    out_sem,
    send_sem,
    recv_sem,
    edge_send,
    edge_recv,
):
    rows = features.shape[0]
    width = enc_weight.shape[1]
    wide = width // LANES
    cap = rows // n
    pieces = cap // LANES
    parts = rows // STEP
    devices = groups * n
    bound = sending_one.shape[1]
    count = devices * bound
    blocks, slots, size = tiles_one.shape[:3]
    per_step = STEP // size
    far_blocks = count // size
    dom, me = lax.axis_index("dom"), lax.axis_index("shard")
    flat = dom * n + me

    def chunk(c):
        return pltpu.make_async_copy(
            features.at[span(c * STEP, STEP), :], feats.at[c % RING], feat_sem.at[c % RING]
        )

    loads = [
        pltpu.make_async_copy(enc_weight, weight, load_sem.at[0]),
        pltpu.make_async_copy(tiles_one, tiles.at[0], load_sem.at[1]),
        pltpu.make_async_copy(tiles_two, tiles.at[1], load_sem.at[2]),
    ] + [
        pltpu.make_async_copy(source, weights.at[i], load_sem.at[3 + i])
        for i, source in enumerate((self_one, neigh_one, self_two, neigh_two))
    ]
    loads[0].start()
    for c in range(RING):
        chunk(c).start()
    barrier = pltpu.get_barrier_semaphore()

    def other(q):
        return (flipped(dom, q // n, groups), flipped(me, q % n, n))

    def greet(q, carry):
        pl.semaphore_signal(barrier, inc=1, device_id=other(q), device_id_type=MESH)
        return carry

    lax.fori_loop(1, devices, greet, 0)
    loads[0].wait()

    def encode(c, carry):
        chunk(c).wait()
        found = jnp.maximum(dot(feats[c % RING], weight[...]), 0.0)
        found = found.astype(jnp.bfloat16).astype(jnp.float32)
        work[span(c * STEP, STEP)] = found.reshape(STEP, wide, LANES)
        return carry

    def encode_more(c, carry):
        encode(c, carry)
        chunk(c + RING).start()
        return carry

    lax.fori_loop(0, parts - RING, encode_more, 0)
    lax.fori_loop(parts - RING, parts, encode, 0)
    pl.semaphore_wait(barrier, devices - 1)

    def gather(read):
        def take(j, carry):
            found = [work[read(j, u)] for u in range(UNROLL)]
            for u in range(UNROLL):
                picked[j * UNROLL + u] = found[u]
            return carry

        lax.fori_loop(0, LANES // UNROLL, take, 0)
        return picked[...].reshape(LANES, width).astype(jnp.bfloat16)

    def peer(w, a):
        return turned(1 + ABREAST * (w // pieces) + a, n)

    def transfer(m, piece):
        at = m * pieces + piece
        return pltpu.make_async_remote_copy(
            src_ref=stage.at[at],
            dst_ref=recv.at[at],
            send_sem=send_sem.at[at],
            recv_sem=recv_sem.at[at],
            device_id=(dom, flipped(me, m, n)),
            device_id_type=MESH,
        )

    def pack_piece(m, piece):
        t = flipped(me, m, n)
        stage[m * pieces + piece] = gather(
            lambda j, u: packing[t, piece * LANES + j * UNROLL + u]
        )

    def pack(w, carry):
        for a in range(ABREAST):
            pack_piece(peer(w, a), w % pieces)
        return carry

    def start(w):
        for a in range(ABREAST):
            transfer(peer(w, a), w % pieces).start()

    def pack_start(w, carry):
        pack(w, carry)
        start(w)
        return carry

    waves = (n - 1) // ABREAST * pieces
    alone = [turned(n - 1 - r, n) for r in range((n - 1) % ABREAST)]
    lax.fori_loop(0, AHEAD, pack_start, 0)
    for m in alone:

        def pack_alone(piece, carry):
            pack_piece(m, piece)
            transfer(m, piece).start()
            return carry

        lax.fori_loop(0, pieces, pack_alone, 0)
    for load in loads[1:]:
        load.start()
    lax.fori_loop(AHEAD, waves, pack, 0)

    def pack_own(piece, carry):
        pack_piece(0, piece)
        return carry

    lax.fori_loop(0, pieces, pack_own, 0)

    lane = lax.broadcasted_iota(jnp.int32, (LANES, LANES), 1)
    for c in range(rows // LANES):
        row = placing_row[0:1, c * LANES : (c + 1) * LANES]
        place_ids[c * LANES : (c + 1) * LANES, :] = (
            jnp.broadcast_to(row, (LANES, LANES)).T - lane
        )
    for c in range(rows // LANES):
        given = degree[c : c + 1, :].astype(jnp.float32)
        share[c * LANES : (c + 1) * LANES, :] = 1.0 / jnp.broadcast_to(given, (LANES, LANES)).T
    line_lane = lax.broadcasted_iota(jnp.int32, (1, LANES), 1)

    def edge_place(e, carry):
        for b in range(bound):
            row = sending_one[e, b]
            slot = placing[0, jnp.minimum(row, rows - 1)]
            slot = jnp.where(row < rows, slot, NOWHERE)
            edge_ids[pl.ds(e * bound + b, 1), :] = jnp.full((1, LANES), slot) - line_lane
        return carry

    lax.fori_loop(0, devices, edge_place, 0)
    zeros = jnp.zeros((size, width), jnp.bfloat16)
    owned[blocks] = zeros
    halo_mixed[far_blocks] = zeros

    def chosen(ids, firsts):
        return jnp.concatenate(
            [jnp.where(ids == first, 1.0, 0.0).astype(jnp.bfloat16) for first in firsts], axis=1
        )

    def place_edge(table, found_at, firsts, fresh):
        def body(r, carry):
            here = span(r * STEP, STEP)
            rhs = jnp.concatenate([table[at] for at in found_at], axis=0)
            found = dot(chosen(edge_ids[here, :], firsts), rhs).astype(jnp.bfloat16)
            edge[0, here, :] = found if fresh else edge[0, here, :] + found
            return carry

        lax.fori_loop(0, count // STEP, body, 0)

    def place(table, found_at, firsts, fresh):
        tall = 2 * STEP

        def body(r, carry):
            here = span(r * tall, tall)
            there = span(r * (tall // size), tall // size)
            rhs = jnp.concatenate([table[at] for at in found_at], axis=0)
            found = dot(chosen(place_ids[here, :], firsts), rhs)
            found = found.astype(jnp.bfloat16).reshape(tall // size, size, width)
            owned[there] = found if fresh else owned[there] + found
            return carry

        lax.fori_loop(0, rows // tall, body, 0)

    def whole_source(m):
        source = flipped(me, m, n) * cap
        return (
            [m * pieces + p for p in range(pieces)],
            [source + p * LANES for p in range(pieces)],
        )

    found_at, firsts = whole_source(0)
    place_edge(stage, found_at, firsts, True)
    place(stage, found_at, firsts, True)
    for m in alone:
        found_at, firsts = whole_source(m)

        def landed(piece, carry):
            transfer(m, piece).wait()
            return carry

        lax.fori_loop(0, pieces, landed, 0)
        place_edge(recv, found_at, firsts, False)
        place(recv, found_at, firsts, False)

    def wave(w):
        piece = w % pieces
        peers = [peer(w, a) for a in range(ABREAST)]
        return (
            [m * pieces + piece for m in peers],
            [flipped(me, m, n) * cap + piece * LANES for m in peers],
        )

    def arrive(w):
        for a in range(ABREAST):
            transfer(peer(w, a), w % pieces).wait()

    def take_wave(w, carry):
        arrive(w)
        start(w + AHEAD)
        found_at, firsts = wave(w)
        place_edge(recv, found_at, firsts, False)
        place(recv, found_at, firsts, False)
        return carry

    def late_wave(w, carry):
        arrive(w)
        found_at, firsts = wave(w)
        place_edge(recv, found_at, firsts, False)
        place(recv, found_at, firsts, False)
        return carry

    lax.fori_loop(0, waves - AHEAD, take_wave, 0)
    lax.fori_loop(waves - AHEAD, waves - 1, late_wave, 0)

    def edge_copy(layer, q):
        to_dom, to_me = other(q)
        to = to_dom * n + to_me
        return pltpu.make_async_remote_copy(
            src_ref=edge.at[layer, span(to * bound, bound), :],
            dst_ref=halo.at[layer, span(flat * bound, bound), :],
            send_sem=edge_send.at[layer, q],
            recv_sem=edge_recv.at[layer, q],
            device_id=(to_dom, to_me),
            device_id_type=MESH,
        )

    def edge_start(layer):
        def send(k, carry):
            edge_copy(layer, devices - k).start()
            return carry

        lax.fori_loop(1, devices, send, 0)
        mine = span(flat * bound, bound)
        halo[layer, mine, :] = edge[layer, mine, :]

    def edge_wait(layer):
        def done(k, carry):
            edge_copy(layer, devices - k).wait()
            return carry

        lax.fori_loop(1, devices, done, 0)

    arrive(waves - 1)
    found_at, firsts = wave(waves - 1)
    place_edge(recv, found_at, firsts, False)
    edge_start(0)
    place(recv, found_at, firsts, False)
    for load in loads[1:]:
        load.wait()
    stage[blocks] = zeros
    work[rows] = jnp.zeros((wide, LANES), jnp.float32)

    def shared(layer, b, table, where):
        lhs = jnp.concatenate([tiles[layer, b, k] for k in range(slots)], axis=1)
        rhs = jnp.concatenate([table[where(b, k)] for k in range(slots)], axis=0)
        part = share[span(b * size, size), :]
        return dot(lhs, rhs) * jnp.concatenate([part] * wide, axis=1)

    def front(layer, source, index, live):
        def near(b, k):
            at = index[k, b]
            return jnp.where((k < live[b]) & (at < blocks), at, blocks)

        def body(step, carry):
            aggregate = jnp.concatenate(
                [
                    shared(layer, step * per_step + j, source, near).astype(jnp.bfloat16)
                    for j in range(per_step)
                ],
                axis=0,
            )
            own = source[span(step * per_step, per_step)].reshape(STEP, width)
            mixed = dot(own, weights[2 * layer]) + dot(aggregate, weights[2 * layer + 1])
            work[span(step * STEP, STEP)] = mixed.reshape(STEP, wide, LANES)
            return carry

        lax.fori_loop(0, parts, body, 0)

    def back(layer, index, live, use):
        def mix(r, carry):
            mixed = dot(halo[layer, span(r * STEP, STEP), :], weights[2 * layer + 1])
            halo_mixed[span(r * per_step, per_step)] = mixed.astype(jnp.bfloat16).reshape(
                per_step, size, width
            )
            return carry

        lax.fori_loop(0, count // STEP, mix, 0)

        def far(b, k):
            at = index[k, b]
            return jnp.where((k < live[b]) & (at >= blocks), at - blocks, far_blocks)

        def body(step, carry):
            mixed = work[span(step * STEP, STEP)].reshape(STEP, width)
            mixed = mixed + jnp.concatenate(
                [shared(layer, step * per_step + j, halo_mixed, far) for j in range(per_step)],
                axis=0,
            )
            active = jnp.maximum(mixed, 0.0)
            scale = lax.rsqrt(jnp.mean(active * active, axis=-1, keepdims=True) + 1e-06)
            use(step, (active * scale).astype(jnp.bfloat16))
            return carry

        lax.fori_loop(0, parts, body, 0)

    front(0, owned, index_one, live_one)
    edge_wait(0)

    def keep(step, result):
        stage[span(step * per_step, per_step)] = result.reshape(per_step, size, width)
        work[span(step * STEP, STEP)] = result.astype(jnp.float32).reshape(STEP, wide, LANES)

    back(0, index_one, live_one, keep)

    def edge_pick(r, carry):
        def read(j, u):
            return sending_two[(r * LANES + j * UNROLL) // bound + u // bound, u % bound]

        edge[1, span(r * LANES, LANES), :] = gather(read)
        return carry

    lax.fori_loop(0, count // LANES, edge_pick, 0)
    edge_start(1)
    front(1, stage, index_two, live_two)
    edge_wait(1)

    def leaving(step):
        here = span(step * STEP, STEP)
        return pltpu.make_async_copy(
            recv.at[span(step * per_step, per_step)],
            embedding.at[span(step * per_step, per_step)],
            out_sem.at[step],
        )

    heads = jnp.broadcast_to(head[...].astype(jnp.float32), (16, width)).astype(jnp.bfloat16)

    def finish(step, result):
        recv[span(step * per_step, per_step)] = result.reshape(per_step, size, width)
        leaving(step).start()
        logits = lax.dot_general(
            heads, result, (((1,), (1,)), ((), ())), preferred_element_type=jnp.float32
        )
        probability[pl.ds(step, 1)] = jax.nn.sigmoid(logits[0:1, :])[None]

    back(1, index_two, live_two, finish)

    def left(step, carry):
        leaving(step).wait()
        return carry

    lax.fori_loop(0, parts, left, 0)


def per_device(
    features,
    enc_weight,
    pack_index,
    place_index,
    halo_send_one,
    halo_send_two,
    tile_index_one,
    tile_index_two,
    tile_live_one,
    tile_live_two,
    tiles_one,
    tiles_two,
    degree,
    self_weight_one,
    neigh_weight_one,
    self_weight_two,
    neigh_weight_two,
    head_weight,
):
    groups, n = lax.axis_size("dom"), lax.axis_size("shard")
    rows, depth = features.shape
    width = enc_weight.shape[1]
    wide = width // LANES
    blocks, slots, size = tiles_one.shape[:3]
    bound = halo_send_one.shape[-1]
    devices = groups * n
    count = devices * bound
    parts = rows // STEP
    cap = rows // n
    vmem = pl.BlockSpec(memory_space=pltpu.VMEM)
    smem = pl.BlockSpec(memory_space=pltpu.SMEM)
    hbm = pl.BlockSpec(memory_space=pl.ANY)
    bf16, f32 = jnp.bfloat16, jnp.float32
    embedding, probability = pl.pallas_call(
        functools.partial(kernel, groups, n),
        out_shape=(
            jax.ShapeDtypeStruct((blocks, size, width), bf16),
            jax.ShapeDtypeStruct((parts, 1, STEP), f32),
        ),
        in_specs=[hbm, hbm, smem, smem, vmem]
        + [smem] * 6
        + [hbm, hbm, vmem]
        + [hbm] * 4
        + [vmem],
        out_specs=(hbm, vmem),
        scratch_shapes=[
            pltpu.VMEM((RING, STEP, depth), bf16),
            pltpu.VMEM((depth, width), bf16),
            pltpu.VMEM((4, width, width), bf16),
            pltpu.VMEM((2, blocks, slots, size, size), bf16),
            pltpu.VMEM((rows + 2, wide, LANES), f32),
            pltpu.VMEM((LANES, wide, LANES), f32),
            pltpu.VMEM((blocks + 1, size, width), bf16),
            pltpu.VMEM((blocks, size, width), bf16),
            pltpu.VMEM((blocks + 1, size, width), bf16),
            pltpu.VMEM((rows, LANES), jnp.int32),
            pltpu.VMEM((count, LANES), jnp.int32),
            pltpu.VMEM((rows, LANES), f32),
            pltpu.VMEM((2, count, width), bf16),
            pltpu.VMEM((2, count, width), bf16),
            pltpu.VMEM((count // size + 1, size, width), bf16),
            pltpu.SemaphoreType.DMA((RING,)),
            pltpu.SemaphoreType.DMA((7,)),
            pltpu.SemaphoreType.DMA((parts,)),
            pltpu.SemaphoreType.DMA((rows // LANES,)),
            pltpu.SemaphoreType.DMA((rows // LANES,)),
            pltpu.SemaphoreType.DMA((2, devices)),
            pltpu.SemaphoreType.DMA((2, devices)),
        ],
        compiler_params=pltpu.CompilerParams(
            collective_id=0, has_side_effects=True, vmem_limit_bytes=VMEM_LIMIT
        ),
        cost_estimate=pl.CostEstimate(
            flops=2 * rows * width * (depth + rows + 4 * slots * size + 4 * width),
            bytes_accessed=rows * depth * 2 + tiles_one.size * 4 + rows * width * 2,
            transcendentals=0,
        ),
    )(
        features,
        enc_weight,
        pack_index.reshape(n, cap),
        place_index.reshape(1, rows),
        place_index.reshape(1, rows),
        halo_send_one.reshape(devices, bound),
        halo_send_two.reshape(devices, bound),
        tile_index_one.T,
        tile_index_two.T,
        tile_live_one,
        tile_live_two,
        tiles_one,
        tiles_two,
        degree.reshape(-1, LANES),
        self_weight_one,
        neigh_weight_one,
        self_weight_two,
        neigh_weight_two,
        head_weight.reshape(1, width),
    )
    return (embedding.reshape(rows, width), probability.reshape(-1))


def solution(mesh):
    placed = (
        P(("dom", "shard"), None),
        P(),
        P("dom", "shard", None, None),
        P("dom", "shard", None),
        P("dom", "shard", None, None, None),
        P("dom", "shard", None, None, None),
        P(("dom", "shard"), None),
        P(("dom", "shard"), None),
        P(("dom", "shard")),
        P(("dom", "shard")),
        P(("dom", "shard"), None, None, None),
        P(("dom", "shard"), None, None, None),
        P(("dom", "shard")),
        P(),
        P(),
        P(),
        P(),
        P(),
    )
    return jax.shard_map(
        per_device,
        mesh=mesh,
        in_specs=placed,
        out_specs=(P(("dom", "shard"), None), P(("dom", "shard"))),
        check_vma=False,
    )
```

```python
import functools

import jax
import jax.numpy as jnp
from jax import lax
from jax.experimental import pallas as pl
from jax.experimental.pallas import tpu as pltpu
from jax.sharding import PartitionSpec as P

LANES = 128
STEP = 512
RING = 4
UNROLL = 32
ABREAST = 3
AHEAD = 3
BACK = 1024
VMEM_LIMIT = 59 << 20
MESH = pl.DeviceIdType.MESH
NOWHERE = -(1 << 20)


def dot(a, b):
    return jnp.dot(a, b, preferred_element_type=jnp.float32)


def span(first, count):
    return pl.ds(pl.multiple_of(first, count), count)


def flipped(a, b, n):
    total, bit = 0, 1
    while bit < n:
        p, q = (a // bit) % 2, (b // bit) % 2
        total = total + bit * (p + q - 2 * p * q)
        bit *= 2
    return total


def turned(step, n):
    half = n // 2
    return jnp.where(step < half, 2 * step, (2 * (step - half) + 3) % n)


def kernel(
    groups,
    n,
    features,
    enc_weight,
    packing,
    placing,
    placing_row,
    sending_one,
    sending_two,
    index_one,
    index_two,
    live_one,
    live_two,
    tiles_one,
    tiles_two,
    degree,
    self_one,
    neigh_one,
    self_two,
    neigh_two,
    head,
    embedding,
    probability,
    feats,
    weight,
    weights,
    tiles,
    work,
    picked,
    stage,
    recv,
    owned,
    place_ids,
    edge_ids,
    share,
    edge,
    halo,
    halo_mixed,
    far_tiles,
    feat_sem,
    load_sem,
    send_sem,
    recv_sem,
    edge_send,
    edge_recv,
):
    rows = features.shape[0]
    width = enc_weight.shape[1]
    wide = width // LANES
    cap = rows // n
    pieces = cap // LANES
    parts = rows // STEP
    devices = groups * n
    bound = sending_one.shape[1]
    count = devices * bound
    blocks, slots, size = tiles_one.shape[:3]
    per_step = STEP // size
    far_blocks = count // size
    dense = far_tiles.shape[1] == rows
    tall = BACK if dense else STEP
    dom, me = lax.axis_index("dom"), lax.axis_index("shard")
    flat = dom * n + me

    def other(q):
        return (flipped(dom, q // n, groups), flipped(me, q % n, n))

    barrier = pltpu.get_barrier_semaphore()
    for away in range(groups):

        def greet(q, carry):
            to = ((dom + away) % groups, (me + q) % n)
            pl.semaphore_signal(barrier, inc=1, device_id=to, device_id_type=MESH)
            return carry

        lax.fori_loop(0 if away else 1, n, greet, 0)

    def chunk(c):
        return pltpu.make_async_copy(
            features.at[span(c * STEP, STEP), :], feats.at[c % RING], feat_sem.at[c % RING]
        )

    loads = [
        pltpu.make_async_copy(enc_weight, weight, load_sem.at[0]),
        pltpu.make_async_copy(tiles_one, tiles.at[0], load_sem.at[1]),
        pltpu.make_async_copy(tiles_two, tiles.at[1], load_sem.at[2]),
    ] + [
        pltpu.make_async_copy(source, weights.at[i], load_sem.at[3 + i])
        for i, source in enumerate((self_one, neigh_one, self_two, neigh_two))
    ]
    loads[0].start()
    for c in range(RING):
        chunk(c).start()
    loads[0].wait()

    def encode(c, carry):
        chunk(c).wait()
        found = jnp.maximum(dot(feats[c % RING], weight[...]), 0.0)
        found = found.astype(jnp.bfloat16).astype(jnp.float32)
        work[span(c * STEP, STEP)] = found.reshape(STEP, wide, LANES)
        return carry

    def encode_more(c, carry):
        encode(c, carry)
        chunk(c + RING).start()
        return carry

    lax.fori_loop(0, parts - RING, encode_more, 0)
    lax.fori_loop(parts - RING, parts, encode, 0)
    pl.semaphore_wait(barrier, devices - 1)

    def gather(read):
        def take(j, carry):
            found = [work[read(j, u)] for u in range(UNROLL)]
            for u in range(UNROLL):
                picked[j * UNROLL + u] = found[u]
            return carry

        lax.fori_loop(0, LANES // UNROLL, take, 0)
        return picked[...].reshape(LANES, width).astype(jnp.bfloat16)

    def peer(w, a):
        return turned(1 + ABREAST * (w // pieces) + a, n)

    def transfer(m, piece):
        at = m * pieces + piece
        return pltpu.make_async_remote_copy(
            src_ref=stage.at[at],
            dst_ref=recv.at[at],
            send_sem=send_sem.at[at],
            recv_sem=recv_sem.at[at],
            device_id=(dom, flipped(me, m, n)),
            device_id_type=MESH,
        )

    def pack_piece(m, piece):
        t = flipped(me, m, n)
        stage[m * pieces + piece] = gather(
            lambda j, u: packing[t, piece * LANES + j * UNROLL + u]
        )

    def pack(w, carry):
        for a in range(ABREAST):
            pack_piece(peer(w, a), w % pieces)
        return carry

    def start(w):
        for a in range(ABREAST):
            transfer(peer(w, a), w % pieces).start()

    def pack_start(w, carry):
        pack(w, carry)
        start(w)
        return carry

    waves = (n - 1) // ABREAST * pieces
    alone = [turned(n - 1 - r, n) for r in range((n - 1) % ABREAST)]
    lax.fori_loop(0, AHEAD, pack_start, 0)
    for m in alone:

        def pack_alone(piece, carry):
            pack_piece(m, piece)
            transfer(m, piece).start()
            return carry

        lax.fori_loop(0, pieces, pack_alone, 0)
    for load in loads[1:]:
        load.start()

    def pack_own(piece, carry):
        pack_piece(0, piece)
        return carry

    lax.fori_loop(0, pieces, pack_own, 0)

    lane = lax.broadcasted_iota(jnp.int32, (LANES, LANES), 1)
    for c in range(rows // LANES):
        row = placing_row[0:1, c * LANES : (c + 1) * LANES]
        place_ids[c * LANES : (c + 1) * LANES, :] = (
            jnp.broadcast_to(row, (LANES, LANES)).T - lane
        )
    for c in range(rows // LANES):
        given = degree[c : c + 1, :].astype(jnp.float32)
        share[c * LANES : (c + 1) * LANES, :] = 1.0 / jnp.broadcast_to(given, (LANES, LANES)).T
    line_lane = lax.broadcasted_iota(jnp.int32, (1, LANES), 1)

    def edge_place(e, carry):
        for b in range(bound):
            row = sending_one[e, b]
            slot = placing[0, jnp.minimum(row, rows - 1)]
            slot = jnp.where(row < rows, slot, NOWHERE)
            edge_ids[pl.ds(e * bound + b, 1), :] = jnp.full((1, LANES), slot) - line_lane
        return carry

    lax.fori_loop(0, devices, edge_place, 0)
    zeros = jnp.zeros((size, width), jnp.bfloat16)
    owned[blocks] = zeros
    halo_mixed[far_blocks] = zeros

    def chosen(ids, firsts):
        return jnp.concatenate(
            [jnp.where(ids == first, 1.0, 0.0).astype(jnp.bfloat16) for first in firsts], axis=1
        )

    def place_edge(table, found_at, firsts, fresh):
        def body(r, carry):
            here = span(r * STEP, STEP)
            rhs = jnp.concatenate([table[at] for at in found_at], axis=0)
            found = dot(chosen(edge_ids[here, :], firsts), rhs).astype(jnp.bfloat16)
            edge[0, here, :] = found if fresh else edge[0, here, :] + found
            return carry

        lax.fori_loop(0, count // STEP, body, 0)

    def place(table, found_at, firsts, fresh):
        tall = 2 * STEP

        def body(r, carry):
            here = span(r * tall, tall)
            there = span(r * (tall // size), tall // size)
            rhs = jnp.concatenate([table[at] for at in found_at], axis=0)
            found = dot(chosen(place_ids[here, :], firsts), rhs)
            found = found.astype(jnp.bfloat16).reshape(tall // size, size, width)
            owned[there] = found if fresh else owned[there] + found
            return carry

        lax.fori_loop(0, rows // tall, body, 0)

    def whole_source(m):
        source = flipped(me, m, n) * cap
        return (
            [m * pieces + p for p in range(pieces)],
            [source + p * LANES for p in range(pieces)],
        )

    found_at, firsts = whole_source(0)
    place_edge(stage, found_at, firsts, True)
    place(stage, found_at, firsts, True)

    def wave(w):
        piece = w % pieces
        peers = [peer(w, a) for a in range(ABREAST)]
        return (
            [m * pieces + piece for m in peers],
            [flipped(me, m, n) * cap + piece * LANES for m in peers],
        )

    def arrive(w):
        for a in range(ABREAST):
            transfer(peer(w, a), w % pieces).wait()

    def take(first, total):
        found_at, firsts = [], []
        for w in range(first, first + total):
            at, source = wave(w)
            found_at, firsts = found_at + at, firsts + source
        place_edge(recv, found_at, firsts, False)
        place(recv, found_at, firsts, False)

    def gather_far(layer, index, live):
        def body(b, carry):
            for f in range(far_blocks):
                total = None
                for k in range(slots):
                    on = (k < live[b]) & (index[k, b] == blocks + f)
                    flag = jnp.where(on, 1.0, 0.0).astype(jnp.float32)
                    term = tiles[layer, b, k] * jnp.full((size, size), flag).astype(jnp.bfloat16)
                    total = term if total is None else total + term
                far_tiles[layer, span(b * size, size), f * size : (f + 1) * size] = total
            return carry

        lax.fori_loop(0, blocks, body, 0)

    paired = (waves - 2) // 2
    for p in range(paired):
        lax.fori_loop(min(2 * p + AHEAD, waves), min(2 * p + AHEAD + 2, waves), pack, 0)
        for w in (2 * p, 2 * p + 1):
            arrive(w)
            if w + AHEAD < waves:
                start(w + AHEAD)
        take(2 * p, 2)
        if p == 0:
            for m in alone:
                found_at, firsts = whole_source(m)

                def landed(piece, carry):
                    transfer(m, piece).wait()
                    return carry

                lax.fori_loop(0, pieces, landed, 0)
                place_edge(recv, found_at, firsts, False)
                place(recv, found_at, firsts, False)
        if p == 1:
            for load in loads[1:]:
                load.wait()
            if dense:
                gather_far(0, index_one, live_one)
                gather_far(1, index_two, live_two)
    for w in range(2 * paired, waves - 1):
        arrive(w)
        take(w, 1)

    def edge_copy(layer, q):
        to_dom, to_me = other(q)
        to = to_dom * n + to_me
        return pltpu.make_async_remote_copy(
            src_ref=edge.at[layer, span(to * bound, bound), :],
            dst_ref=halo.at[layer, span(flat * bound, bound), :],
            send_sem=edge_send.at[layer, q],
            recv_sem=edge_recv.at[layer, q],
            device_id=(to_dom, to_me),
            device_id_type=MESH,
        )

    def edge_start(layer):
        def send(k, carry):
            edge_copy(layer, devices - k).start()
            return carry

        lax.fori_loop(1, devices, send, 0)
        mine = span(flat * bound, bound)
        halo[layer, mine, :] = edge[layer, mine, :]

    def edge_wait(layer):
        def done(k, carry):
            edge_copy(layer, devices - k).wait()
            return carry

        lax.fori_loop(1, devices, done, 0)

    arrive(waves - 1)
    found_at, firsts = wave(waves - 1)
    place_edge(recv, found_at, firsts, False)
    edge_start(0)
    place(recv, found_at, firsts, False)
    stage[blocks] = zeros
    work[rows] = jnp.zeros((wide, LANES), jnp.float32)

    def shared(layer, b, table, where):
        lhs = jnp.concatenate([tiles[layer, b, k] for k in range(slots)], axis=1)
        rhs = jnp.concatenate([table[where(b, k)] for k in range(slots)], axis=0)
        part = share[span(b * size, size), :]
        return dot(lhs, rhs) * jnp.concatenate([part] * wide, axis=1)

    def front(layer, source, index, live):
        def near(b, k):
            at = index[k, b]
            return jnp.where((k < live[b]) & (at < blocks), at, blocks)

        def body(step, carry):
            aggregate = jnp.concatenate(
                [
                    shared(layer, step * per_step + j, source, near).astype(jnp.bfloat16)
                    for j in range(per_step)
                ],
                axis=0,
            )
            own = source[span(step * per_step, per_step)].reshape(STEP, width)
            mixed = dot(own, weights[2 * layer]) + dot(aggregate, weights[2 * layer + 1])
            work[span(step * STEP, STEP)] = mixed.reshape(STEP, wide, LANES)
            return carry

        lax.fori_loop(0, parts, body, 0)

    def back(layer, index, live, use):
        def mix(r, carry):
            mixed = dot(halo[layer, span(r * STEP, STEP), :], weights[2 * layer + 1])
            halo_mixed[span(r * per_step, per_step)] = mixed.astype(jnp.bfloat16).reshape(
                per_step, size, width
            )
            return carry

        lax.fori_loop(0, count // STEP, mix, 0)

        def far(b, k):
            at = index[k, b]
            return jnp.where((k < live[b]) & (at >= blocks), at - blocks, far_blocks)

        def body(step, carry):
            here = span(step * tall, tall)
            mixed = work[here].reshape(tall, width)
            if dense:
                table = halo_mixed[0:far_blocks].reshape(count, width)
                part = jnp.concatenate([share[here, :]] * wide, axis=1)
                mixed = mixed + dot(far_tiles[layer, here, :], table) * part
            else:
                mixed = mixed + jnp.concatenate(
                    [shared(layer, step * per_step + j, halo_mixed, far) for j in range(per_step)],
                    axis=0,
                )
            active = jnp.maximum(mixed, 0.0)
            scale = lax.rsqrt(jnp.mean(active * active, axis=-1, keepdims=True) + 1e-06)
            use(step, (active * scale).astype(jnp.bfloat16))
            return carry

        lax.fori_loop(0, rows // tall, body, 0)

    front(0, owned, index_one, live_one)
    edge_wait(0)

    def keep(step, result):
        stage[span(step * (tall // size), tall // size)] = result.reshape(-1, size, width)
        work[span(step * tall, tall)] = result.astype(jnp.float32).reshape(tall, wide, LANES)

    back(0, index_one, live_one, keep)

    def edge_pick(r, carry):
        def read(j, u):
            return sending_two[(r * LANES + j * UNROLL) // bound + u // bound, u % bound]

        edge[1, span(r * LANES, LANES), :] = gather(read)
        return carry

    lax.fori_loop(0, count // LANES, edge_pick, 0)
    edge_start(1)
    front(1, stage, index_two, live_two)
    edge_wait(1)

    heads = jnp.broadcast_to(head[...].astype(jnp.float32), (16, width)).astype(jnp.bfloat16)

    def finish(step, result):
        embedding[span(step * (tall // size), tall // size)] = result.reshape(-1, size, width)
        logits = lax.dot_general(
            heads, result, (((1,), (1,)), ((), ())), preferred_element_type=jnp.float32
        )
        probability[pl.ds(step, 1)] = jax.nn.sigmoid(logits[0:1, :])[None]

    back(1, index_two, live_two, finish)


def per_device(
    features,
    enc_weight,
    pack_index,
    place_index,
    halo_send_one,
    halo_send_two,
    tile_index_one,
    tile_index_two,
    tile_live_one,
    tile_live_two,
    tiles_one,
    tiles_two,
    degree,
    self_weight_one,
    neigh_weight_one,
    self_weight_two,
    neigh_weight_two,
    head_weight,
):
    groups, n = lax.axis_size("dom"), lax.axis_size("shard")
    rows, depth = features.shape
    width = enc_weight.shape[1]
    wide = width // LANES
    blocks, slots, size = tiles_one.shape[:3]
    bound = halo_send_one.shape[-1]
    devices = groups * n
    count = devices * bound
    cap = rows // n
    dense = count <= rows // 8
    tall = BACK if dense else STEP
    vmem = pl.BlockSpec(memory_space=pltpu.VMEM)
    smem = pl.BlockSpec(memory_space=pltpu.SMEM)
    hbm = pl.BlockSpec(memory_space=pl.ANY)
    bf16, f32 = jnp.bfloat16, jnp.float32
    embedding, probability = pl.pallas_call(
        functools.partial(kernel, groups, n),
        out_shape=(
            pltpu.VMEM((blocks, size, width), bf16),
            jax.ShapeDtypeStruct((rows // tall, 1, tall), f32),
        ),
        in_specs=[hbm, hbm, smem, smem, vmem]
        + [smem] * 6
        + [hbm, hbm, vmem]
        + [hbm] * 4
        + [vmem],
        out_specs=(vmem, vmem),
        scratch_shapes=[
            pltpu.VMEM((RING, STEP, depth), bf16),
            pltpu.VMEM((depth, width), bf16),
            pltpu.VMEM((4, width, width), bf16),
            pltpu.VMEM((2, blocks, slots, size, size), bf16),
            pltpu.VMEM((rows + 2, wide, LANES), f32),
            pltpu.VMEM((LANES, wide, LANES), f32),
            pltpu.VMEM((blocks + 1, size, width), bf16),
            pltpu.VMEM((blocks, size, width), bf16),
            pltpu.VMEM((blocks + 1, size, width), bf16),
            pltpu.VMEM((rows, LANES), jnp.int32),
            pltpu.VMEM((count, LANES), jnp.int32),
            pltpu.VMEM((rows, LANES), f32),
            pltpu.VMEM((2, count, width), bf16),
            pltpu.VMEM((2, count, width), bf16),
            pltpu.VMEM((count // size + 1, size, width), bf16),
            pltpu.VMEM((2, rows if dense else size, count), bf16),
            pltpu.SemaphoreType.DMA((RING,)),
            pltpu.SemaphoreType.DMA((7,)),
            pltpu.SemaphoreType.DMA((rows // LANES,)),
            pltpu.SemaphoreType.DMA((rows // LANES,)),
            pltpu.SemaphoreType.DMA((2, devices)),
            pltpu.SemaphoreType.DMA((2, devices)),
        ],
        compiler_params=pltpu.CompilerParams(
            collective_id=0, has_side_effects=True, vmem_limit_bytes=VMEM_LIMIT
        ),
        cost_estimate=pl.CostEstimate(
            flops=2 * rows * width * (depth + rows + 4 * slots * size + 4 * width),
            bytes_accessed=rows * depth * 2 + tiles_one.size * 4 + rows * width * 2,
            transcendentals=0,
        ),
    )(
        features,
        enc_weight,
        pack_index.reshape(n, cap),
        place_index.reshape(1, rows),
        place_index.reshape(1, rows),
        halo_send_one.reshape(devices, bound),
        halo_send_two.reshape(devices, bound),
        tile_index_one.T,
        tile_index_two.T,
        tile_live_one,
        tile_live_two,
        tiles_one,
        tiles_two,
        degree.reshape(-1, LANES),
        self_weight_one,
        neigh_weight_one,
        self_weight_two,
        neigh_weight_two,
        head_weight,
    )
    return (embedding.reshape(rows, width), probability.reshape(-1))


def solution(mesh):
    placed = (
        P(("dom", "shard"), None),
        P(),
        P("dom", "shard", None, None),
        P("dom", "shard", None),
        P("dom", "shard", None, None, None),
        P("dom", "shard", None, None, None),
        P(("dom", "shard"), None),
        P(("dom", "shard"), None),
        P(("dom", "shard")),
        P(("dom", "shard")),
        P(("dom", "shard"), None, None, None),
        P(("dom", "shard"), None, None, None),
        P(("dom", "shard")),
        P(),
        P(),
        P(),
        P(),
        P(),
    )
    return jax.shard_map(
        per_device,
        mesh=mesh,
        in_specs=placed,
        out_specs=(P(("dom", "shard"), None), P(("dom", "shard"))),
        check_vma=False,
    )
```

```python
import functools

import jax
import jax.numpy as jnp
from jax import lax
from jax.experimental import pallas as pl
from jax.experimental.pallas import tpu as pltpu
from jax.sharding import PartitionSpec as P

LANES = 128
STEP = 512
RING = 4
UNROLL = 32
ABREAST = 3
AHEAD = 3
BACK = 1024
VMEM_LIMIT = 59 << 20
MESH = pl.DeviceIdType.MESH
NOWHERE = -(1 << 20)


def dot(a, b):
    return jnp.dot(a, b, preferred_element_type=jnp.float32)


def span(first, count):
    return pl.ds(pl.multiple_of(first, count), count)


def flipped(a, b, n):
    total, bit = 0, 1
    while bit < n:
        p, q = (a // bit) % 2, (b // bit) % 2
        total = total + bit * (p + q - 2 * p * q)
        bit *= 2
    return total


def turned(step, n):
    half = n // 2
    return jnp.where(step < half, 2 * step, (2 * (step - half) + 3) % n)


def kernel(
    groups,
    n,
    features,
    enc_weight,
    tiles_one,
    tiles_two,
    self_one,
    neigh_one,
    self_two,
    neigh_two,
    packing_in,
    placing_in,
    placing_row_in,
    sending_one_in,
    sending_two_in,
    index_one_in,
    index_two_in,
    live_one_in,
    live_two_in,
    degree_in,
    head_in,
    embedding,
    probability,
    feats,
    weight,
    weights,
    tiles,
    work,
    picked,
    stage,
    recv,
    owned,
    place_ids,
    edge_ids,
    share,
    edge,
    halo,
    halo_mixed,
    far_tiles,
    packing,
    placing,
    placing_row,
    sending_one,
    sending_two,
    index_one,
    index_two,
    live_one,
    live_two,
    degree,
    head,
    small_sem,
    feat_sem,
    load_sem,
    send_sem,
    recv_sem,
    edge_send,
    edge_recv,
):
    rows = features.shape[0]
    width = enc_weight.shape[1]
    wide = width // LANES
    cap = rows // n
    pieces = cap // LANES
    parts = rows // STEP
    devices = groups * n
    bound = sending_one.shape[1]
    count = devices * bound
    blocks, slots, size = tiles_one.shape[:3]
    per_step = STEP // size
    far_blocks = count // size
    dense = far_tiles.shape[1] == rows
    tall = BACK if dense else STEP
    dom, me = lax.axis_index("dom"), lax.axis_index("shard")
    flat = dom * n + me

    barrier = pltpu.get_barrier_semaphore()
    for away in range(groups):

        def greet(q, carry):
            to = ((dom + away) % groups, (me + q) % n)
            pl.semaphore_signal(barrier, inc=1, device_id=to, device_id_type=MESH)
            return carry

        lax.fori_loop(0 if away else 1, n, greet, 0)

    def chunk(c):
        return pltpu.make_async_copy(
            features.at[span(c * STEP, STEP), :], feats.at[c % RING], feat_sem.at[c % RING]
        )

    loads = [
        pltpu.make_async_copy(enc_weight, weight, load_sem.at[0]),
        pltpu.make_async_copy(tiles_one, tiles.at[0], load_sem.at[1]),
        pltpu.make_async_copy(tiles_two, tiles.at[1], load_sem.at[2]),
    ] + [
        pltpu.make_async_copy(source, weights.at[i], load_sem.at[3 + i])
        for i, source in enumerate((self_one, neigh_one, self_two, neigh_two))
    ]
    smalls = [
        pltpu.make_async_copy(source, target, small_sem.at[i])
        for i, (source, target) in enumerate(
            (
                (packing_in, packing),
                (placing_in, placing),
                (placing_row_in, placing_row),
                (sending_one_in, sending_one),
                (sending_two_in, sending_two),
                (index_one_in, index_one),
                (index_two_in, index_two),
                (live_one_in, live_one),
                (live_two_in, live_two),
                (degree_in, degree),
                (head_in, head),
            )
        )
    ]
    loads[0].start()
    for c in range(RING):
        chunk(c).start()
    for copy in smalls:
        copy.start()
    loads[0].wait()

    def encode(c, carry):
        chunk(c).wait()
        found = jnp.maximum(dot(feats[c % RING], weight[...]), 0.0)
        found = found.astype(jnp.bfloat16).astype(jnp.float32)
        work[span(c * STEP, STEP)] = found.reshape(STEP, wide, LANES)
        return carry

    def encode_more(c, carry):
        encode(c, carry)
        chunk(c + RING).start()
        return carry

    lax.fori_loop(0, parts - RING, encode_more, 0)
    lax.fori_loop(parts - RING, parts, encode, 0)
    for copy in smalls:
        copy.wait()
    pl.semaphore_wait(barrier, devices - 1)

    def gather(read):
        def take(j, carry):
            found = [work[read(j, u)] for u in range(UNROLL)]
            for u in range(UNROLL):
                picked[j * UNROLL + u] = found[u]
            return carry

        lax.fori_loop(0, LANES // UNROLL, take, 0)
        return picked[...].reshape(LANES, width).astype(jnp.bfloat16)

    def peer(w, a):
        return turned(1 + ABREAST * (w // pieces) + a, n)

    def transfer(m, piece):
        at = m * pieces + piece
        return pltpu.make_async_remote_copy(
            src_ref=stage.at[at],
            dst_ref=recv.at[at],
            send_sem=send_sem.at[at],
            recv_sem=recv_sem.at[at],
            device_id=(dom, flipped(me, m, n)),
            device_id_type=MESH,
        )

    def pack_piece(m, piece):
        t = flipped(me, m, n)
        stage[m * pieces + piece] = gather(
            lambda j, u: packing[t, piece * LANES + j * UNROLL + u]
        )

    def pack(w, carry):
        for a in range(ABREAST):
            pack_piece(peer(w, a), w % pieces)
        return carry

    def start(w):
        for a in range(ABREAST):
            transfer(peer(w, a), w % pieces).start()

    def pack_start(w, carry):
        for a in range(ABREAST):
            pack_piece(peer(w, a), w % pieces)
            transfer(peer(w, a), w % pieces).start()
        return carry

    waves = (n - 1) // ABREAST * pieces
    alone = [turned(n - 1 - r, n) for r in range((n - 1) % ABREAST)]
    lax.fori_loop(0, AHEAD, pack_start, 0)
    for m in alone:

        def pack_alone(piece, carry):
            pack_piece(m, piece)
            transfer(m, piece).start()
            return carry

        lax.fori_loop(0, pieces, pack_alone, 0)
    for load in loads[1:]:
        load.start()

    def pack_own(piece, carry):
        pack_piece(0, piece)
        return carry

    lax.fori_loop(0, pieces, pack_own, 0)

    lane = lax.broadcasted_iota(jnp.int32, (LANES, LANES), 1)
    for c in range(rows // LANES):
        row = placing_row[0:1, c * LANES : (c + 1) * LANES]
        place_ids[c * LANES : (c + 1) * LANES, :] = (
            jnp.broadcast_to(row, (LANES, LANES)).T - lane
        )
    for c in range(rows // LANES):
        given = degree[c : c + 1, :].astype(jnp.float32)
        share[c * LANES : (c + 1) * LANES, :] = 1.0 / jnp.broadcast_to(given, (LANES, LANES)).T
    line_lane = lax.broadcasted_iota(jnp.int32, (1, LANES), 1)

    def edge_place(e, carry):
        for b in range(bound):
            row = sending_one[e, b]
            slot = placing[0, jnp.minimum(row, rows - 1)]
            slot = jnp.where(row < rows, slot, NOWHERE)
            edge_ids[pl.ds(e * bound + b, 1), :] = jnp.full((1, LANES), slot) - line_lane
        return carry

    lax.fori_loop(0, devices, edge_place, 0)
    zeros = jnp.zeros((size, width), jnp.bfloat16)
    owned[blocks] = zeros
    halo_mixed[far_blocks] = zeros

    def chosen(ids, firsts):
        return jnp.concatenate(
            [jnp.where(ids == first, 1.0, 0.0).astype(jnp.bfloat16) for first in firsts], axis=1
        )

    def place_edge(table, found_at, firsts, fresh):
        def body(r, carry):
            here = span(r * STEP, STEP)
            rhs = jnp.concatenate([table[at] for at in found_at], axis=0)
            found = dot(chosen(edge_ids[here, :], firsts), rhs).astype(jnp.bfloat16)
            edge[0, here, :] = found if fresh else edge[0, here, :] + found
            return carry

        lax.fori_loop(0, count // STEP, body, 0)

    def place(table, found_at, firsts, fresh):
        tall = 2 * STEP

        def body(r, carry):
            here = span(r * tall, tall)
            there = span(r * (tall // size), tall // size)
            rhs = jnp.concatenate([table[at] for at in found_at], axis=0)
            found = dot(chosen(place_ids[here, :], firsts), rhs)
            found = found.astype(jnp.bfloat16).reshape(tall // size, size, width)
            owned[there] = found if fresh else owned[there] + found
            return carry

        lax.fori_loop(0, rows // tall, body, 0)

    def whole_source(m):
        source = flipped(me, m, n) * cap
        return (
            [m * pieces + p for p in range(pieces)],
            [source + p * LANES for p in range(pieces)],
        )

    found_at, firsts = whole_source(0)
    place_edge(stage, found_at, firsts, True)
    place(stage, found_at, firsts, True)

    def wave(w):
        piece = w % pieces
        peers = [peer(w, a) for a in range(ABREAST)]
        return (
            [m * pieces + piece for m in peers],
            [flipped(me, m, n) * cap + piece * LANES for m in peers],
        )

    def arrive(w):
        for a in range(ABREAST):
            transfer(peer(w, a), w % pieces).wait()

    def take(first, total):
        found_at, firsts = [], []
        for w in range(first, first + total):
            at, source = wave(w)
            found_at, firsts = found_at + at, firsts + source
        place_edge(recv, found_at, firsts, False)
        place(recv, found_at, firsts, False)

    def gather_far(layer, index, live):
        def body(b, carry):
            for f in range(far_blocks):
                total = None
                for k in range(slots):
                    on = (k < live[b]) & (index[k, b] == blocks + f)
                    flag = jnp.where(on, 1.0, 0.0).astype(jnp.float32)
                    term = tiles[layer, b, k] * jnp.full((size, size), flag).astype(jnp.bfloat16)
                    total = term if total is None else total + term
                far_tiles[layer, span(b * size, size), f * size : (f + 1) * size] = total
            return carry

        lax.fori_loop(0, blocks, body, 0)

    paired = (waves - 2) // 2
    for p in range(paired):
        lax.fori_loop(min(2 * p + AHEAD, waves), min(2 * p + AHEAD + 2, waves), pack, 0)
        for w in (2 * p, 2 * p + 1):
            arrive(w)
            if w + AHEAD < waves:
                start(w + AHEAD)
        take(2 * p, 2)
        if p == 0:
            for m in alone:
                found_at, firsts = whole_source(m)

                def landed(piece, carry):
                    transfer(m, piece).wait()
                    return carry

                lax.fori_loop(0, pieces, landed, 0)
                place_edge(recv, found_at, firsts, False)
                place(recv, found_at, firsts, False)
        if p == 1:
            for load in loads[1:]:
                load.wait()
            if dense:
                gather_far(0, index_one, live_one)
                gather_far(1, index_two, live_two)
    for w in range(2 * paired, waves - 1):
        arrive(w)
        take(w, 1)

    def edge_start(layer):
        for away in [groups // 2] + [a for a in range(1, groups) if a != groups // 2] + [0]:
            to_dom = (dom + away) % groups
            for q in range(0 if away else 1, n):
                to_me = (me + q) % n
                pltpu.make_async_remote_copy(
                    src_ref=edge.at[layer, span((to_dom * n + to_me) * bound, bound), :],
                    dst_ref=halo.at[layer, span(flat * bound, bound), :],
                    send_sem=edge_send.at[layer],
                    recv_sem=edge_recv.at[layer],
                    device_id=(to_dom, to_me),
                    device_id_type=MESH,
                ).start()
        mine = span(flat * bound, bound)
        halo[layer, mine, :] = edge[layer, mine, :]

    def edge_wait(layer):
        most = pl.ds(0, count - bound)
        for sem in (edge_recv, edge_send):
            pltpu.make_async_copy(
                edge.at[layer, most, :], halo.at[layer, most, :], sem.at[layer]
            ).wait()

    arrive(waves - 1)
    found_at, firsts = wave(waves - 1)
    place_edge(recv, found_at, firsts, False)
    edge_start(0)
    place(recv, found_at, firsts, False)
    stage[blocks] = zeros
    work[rows] = jnp.zeros((wide, LANES), jnp.float32)

    def shared(layer, b, table, where):
        lhs = jnp.concatenate([tiles[layer, b, k] for k in range(slots)], axis=1)
        rhs = jnp.concatenate([table[where(b, k)] for k in range(slots)], axis=0)
        part = share[span(b * size, size), :]
        return dot(lhs, rhs) * jnp.concatenate([part] * wide, axis=1)

    def front(layer, source, index, live):
        def near(b, k):
            at = index[k, b]
            return jnp.where((k < live[b]) & (at < blocks), at, blocks)

        def body(step, carry):
            aggregate = jnp.concatenate(
                [
                    shared(layer, step * per_step + j, source, near).astype(jnp.bfloat16)
                    for j in range(per_step)
                ],
                axis=0,
            )
            own = source[span(step * per_step, per_step)].reshape(STEP, width)
            mixed = dot(own, weights[2 * layer]) + dot(aggregate, weights[2 * layer + 1])
            work[span(step * STEP, STEP)] = mixed.reshape(STEP, wide, LANES)
            return carry

        lax.fori_loop(0, parts, body, 0)

    def back(layer, index, live, use):
        def mix(r, carry):
            mixed = dot(halo[layer, span(r * STEP, STEP), :], weights[2 * layer + 1])
            halo_mixed[span(r * per_step, per_step)] = mixed.astype(jnp.bfloat16).reshape(
                per_step, size, width
            )
            return carry

        lax.fori_loop(0, count // STEP, mix, 0)

        def far(b, k):
            at = index[k, b]
            return jnp.where((k < live[b]) & (at >= blocks), at - blocks, far_blocks)

        def body(step, carry):
            here = span(step * tall, tall)
            mixed = work[here].reshape(tall, width)
            if dense:
                table = halo_mixed[0:far_blocks].reshape(count, width)
                part = jnp.concatenate([share[here, :]] * wide, axis=1)
                mixed = mixed + dot(far_tiles[layer, here, :], table) * part
            else:
                mixed = mixed + jnp.concatenate(
                    [shared(layer, step * per_step + j, halo_mixed, far) for j in range(per_step)],
                    axis=0,
                )
            active = jnp.maximum(mixed, 0.0)
            scale = lax.rsqrt(jnp.mean(active * active, axis=-1, keepdims=True) + 1e-06)
            use(step, (active * scale).astype(jnp.bfloat16))
            return carry

        lax.fori_loop(0, rows // tall, body, 0)

    front(0, owned, index_one, live_one)
    edge_wait(0)

    def keep(step, result):
        stage[span(step * (tall // size), tall // size)] = result.reshape(-1, size, width)
        work[span(step * tall, tall)] = result.astype(jnp.float32).reshape(tall, wide, LANES)

    back(0, index_one, live_one, keep)

    def edge_pick(r, carry):
        def read(j, u):
            return sending_two[(r * LANES + j * UNROLL) // bound + u // bound, u % bound]

        edge[1, span(r * LANES, LANES), :] = gather(read)
        return carry

    lax.fori_loop(0, count // LANES, edge_pick, 0)
    edge_start(1)
    front(1, stage, index_two, live_two)
    edge_wait(1)

    heads = jnp.broadcast_to(head[...].astype(jnp.float32), (16, width)).astype(jnp.bfloat16)

    def finish(step, result):
        embedding[span(step * (tall // size), tall // size)] = result.reshape(-1, size, width)
        logits = lax.dot_general(
            heads, result, (((1,), (1,)), ((), ())), preferred_element_type=jnp.float32
        )
        probability[pl.ds(step, 1)] = jax.nn.sigmoid(logits[0:1, :])[None]

    back(1, index_two, live_two, finish)


def per_device(
    features,
    enc_weight,
    pack_index,
    place_index,
    halo_send_one,
    halo_send_two,
    tile_index_one,
    tile_index_two,
    tile_live_one,
    tile_live_two,
    tiles_one,
    tiles_two,
    degree,
    self_weight_one,
    neigh_weight_one,
    self_weight_two,
    neigh_weight_two,
    head_weight,
):
    groups, n = lax.axis_size("dom"), lax.axis_size("shard")
    rows, depth = features.shape
    width = enc_weight.shape[1]
    wide = width // LANES
    blocks, slots, size = tiles_one.shape[:3]
    bound = halo_send_one.shape[-1]
    devices = groups * n
    count = devices * bound
    cap = rows // n
    dense = count <= rows // 8
    tall = BACK if dense else STEP
    vmem = pl.BlockSpec(memory_space=pltpu.VMEM)
    hbm = pl.BlockSpec(memory_space=pl.ANY)
    bf16, f32, i32 = jnp.bfloat16, jnp.float32, jnp.int32
    embedding, probability = pl.pallas_call(
        functools.partial(kernel, groups, n),
        out_shape=(
            pltpu.VMEM((blocks, size, width), bf16),
            jax.ShapeDtypeStruct((rows // tall, 1, tall), f32),
        ),
        in_specs=[hbm] * 19,
        out_specs=(vmem, vmem),
        scratch_shapes=[
            pltpu.VMEM((RING, STEP, depth), bf16),
            pltpu.VMEM((depth, width), bf16),
            pltpu.VMEM((4, width, width), bf16),
            pltpu.VMEM((2, blocks, slots, size, size), bf16),
            pltpu.VMEM((rows + 2, wide, LANES), f32),
            pltpu.VMEM((LANES, wide, LANES), f32),
            pltpu.VMEM((blocks + 1, size, width), bf16),
            pltpu.VMEM((blocks, size, width), bf16),
            pltpu.VMEM((blocks + 1, size, width), bf16),
            pltpu.VMEM((rows, LANES), jnp.int32),
            pltpu.VMEM((count, LANES), jnp.int32),
            pltpu.VMEM((rows, LANES), f32),
            pltpu.VMEM((2, count, width), bf16),
            pltpu.VMEM((2, count, width), bf16),
            pltpu.VMEM((count // size + 1, size, width), bf16),
            pltpu.VMEM((2, rows if dense else size, count), bf16),
            pltpu.SMEM((n, cap), i32),
            pltpu.SMEM((1, rows), i32),
            pltpu.VMEM((1, rows), i32),
            pltpu.SMEM((devices, bound), i32),
            pltpu.SMEM((devices, bound), i32),
            pltpu.SMEM((slots, blocks), i32),
            pltpu.SMEM((slots, blocks), i32),
            pltpu.SMEM((blocks,), i32),
            pltpu.SMEM((blocks,), i32),
            pltpu.VMEM((rows // LANES, LANES), i32),
            pltpu.VMEM((width,), bf16),
            pltpu.SemaphoreType.DMA((11,)),
            pltpu.SemaphoreType.DMA((RING,)),
            pltpu.SemaphoreType.DMA((7,)),
            pltpu.SemaphoreType.DMA((rows // LANES,)),
            pltpu.SemaphoreType.DMA((rows // LANES,)),
            pltpu.SemaphoreType.DMA((2,)),
            pltpu.SemaphoreType.DMA((2,)),
        ],
        compiler_params=pltpu.CompilerParams(
            collective_id=0, has_side_effects=True, vmem_limit_bytes=VMEM_LIMIT
        ),
        cost_estimate=pl.CostEstimate(
            flops=2 * rows * width * (depth + rows + 4 * slots * size + 4 * width),
            bytes_accessed=rows * depth * 2 + tiles_one.size * 4 + rows * width * 2,
            transcendentals=0,
        ),
    )(
        features,
        enc_weight,
        tiles_one,
        tiles_two,
        self_weight_one,
        neigh_weight_one,
        self_weight_two,
        neigh_weight_two,
        pack_index.reshape(n, cap),
        place_index.reshape(1, rows),
        place_index.reshape(1, rows),
        halo_send_one.reshape(devices, bound),
        halo_send_two.reshape(devices, bound),
        tile_index_one.T,
        tile_index_two.T,
        tile_live_one,
        tile_live_two,
        degree.reshape(-1, LANES),
        head_weight,
    )
    return (embedding.reshape(rows, width), probability.reshape(-1))


def solution(mesh):
    placed = (
        P(("dom", "shard"), None),
        P(),
        P("dom", "shard", None, None),
        P("dom", "shard", None),
        P("dom", "shard", None, None, None),
        P("dom", "shard", None, None, None),
        P(("dom", "shard"), None),
        P(("dom", "shard"), None),
        P(("dom", "shard")),
        P(("dom", "shard")),
        P(("dom", "shard"), None, None, None),
        P(("dom", "shard"), None, None, None),
        P(("dom", "shard")),
        P(),
        P(),
        P(),
        P(),
        P(),
    )
    return jax.shard_map(
        per_device,
        mesh=mesh,
        in_specs=placed,
        out_specs=(P(("dom", "shard"), None), P(("dom", "shard"))),
        check_vma=False,
    )
```

```python
import functools

import jax
import jax.numpy as jnp
from jax import lax
from jax.experimental import pallas as pl
from jax.experimental.pallas import tpu as pltpu
from jax.sharding import PartitionSpec as P

LANES = 128
STEP = 512
RING = 4
UNROLL = 64
ABREAST = 3
AHEAD = 3
BACK = 1024
VMEM_LIMIT = 59 << 20
FIRST_LIMIT = 42 << 20
LAST_LIMIT = 16 << 20
MESH = pl.DeviceIdType.MESH
NOWHERE = -(1 << 20)


def dot(a, b):
    return jnp.dot(a, b, preferred_element_type=jnp.float32)


def span(first, count):
    return pl.ds(pl.multiple_of(first, count), count)


def flipped(a, b, n):
    total, bit = 0, 1
    while bit < n:
        p, q = (a // bit) % 2, (b // bit) % 2
        total = total + bit * (p + q - 2 * p * q)
        bit *= 2
    return total


def turned(step, n):
    half = n // 2
    return jnp.where(step < half, 2 * step, (2 * (step - half) + 3) % n)


def normal(mixed):
    active = jnp.maximum(mixed, 0.0)
    scale = lax.rsqrt(jnp.mean(active * active, axis=-1, keepdims=True) + 1e-06)
    return (active * scale).astype(jnp.bfloat16)


def kernel(
    groups,
    n,
    features,
    enc_weight,
    tiles_one,
    tiles_two,
    self_one,
    neigh_one,
    self_two,
    neigh_two,
    packing_in,
    placing_in,
    placing_row_in,
    sending_one_in,
    sending_two_in,
    index_one_in,
    index_two_in,
    live_one_in,
    live_two_in,
    degree_in,
    head_in,
    embedding,
    probability,
    feats,
    weight,
    weights,
    tiles,
    work,
    picked,
    stage,
    recv,
    owned,
    place_ids,
    edge_ids,
    share,
    edge,
    halo,
    halo_mixed,
    far_tiles,
    packing,
    placing,
    placing_row,
    sending_one,
    sending_two,
    index_one,
    index_two,
    live_one,
    live_two,
    degree,
    head,
    small_sem,
    feat_sem,
    load_sem,
    send_sem,
    recv_sem,
    edge_send,
    edge_recv,
):
    rows = features.shape[0]
    width = enc_weight.shape[1]
    wide = width // LANES
    cap = rows // n
    pieces = cap // LANES
    parts = rows // STEP
    devices = groups * n
    bound = sending_one.shape[1]
    count = devices * bound
    blocks, slots, size = tiles_one.shape[:3]
    per_step = STEP // size
    far_blocks = count // size
    dense = far_tiles.shape[1] == rows
    tall = BACK if dense else STEP
    dom, me = lax.axis_index("dom"), lax.axis_index("shard")
    flat = dom * n + me

    barrier = pltpu.get_barrier_semaphore()
    for away in range(groups):

        def greet(q, carry):
            to = ((dom + away) % groups, (me + q) % n)
            pl.semaphore_signal(barrier, inc=1, device_id=to, device_id_type=MESH)
            return carry

        lax.fori_loop(0 if away else 1, n, greet, 0)

    def chunk(c):
        return pltpu.make_async_copy(
            features.at[span(c * STEP, STEP), :], feats.at[c % RING], feat_sem.at[c % RING]
        )

    loads = [
        pltpu.make_async_copy(enc_weight, weight, load_sem.at[0]),
        pltpu.make_async_copy(tiles_one, tiles.at[0], load_sem.at[1]),
        pltpu.make_async_copy(tiles_two, tiles.at[1], load_sem.at[2]),
    ] + [
        pltpu.make_async_copy(source, weights.at[i], load_sem.at[3 + i])
        for i, source in enumerate((self_one, neigh_one, self_two, neigh_two))
    ]
    smalls = [
        pltpu.make_async_copy(source, target, small_sem.at[i])
        for i, (source, target) in enumerate(
            (
                (packing_in, packing),
                (placing_in, placing),
                (placing_row_in, placing_row),
                (sending_one_in, sending_one),
                (sending_two_in, sending_two),
                (index_one_in, index_one),
                (index_two_in, index_two),
                (live_one_in, live_one),
                (live_two_in, live_two),
                (degree_in, degree),
                (head_in, head),
            )
        )
    ]
    loads[0].start()
    for c in range(RING):
        chunk(c).start()
    for copy in smalls:
        copy.start()
    loads[0].wait()

    def encode(c, carry):
        chunk(c).wait()
        found = jnp.maximum(dot(feats[c % RING], weight[...]), 0.0)
        found = found.astype(jnp.bfloat16).astype(jnp.float32)
        work[span(c * STEP, STEP)] = found.reshape(STEP, wide, LANES)
        return carry

    def encode_more(c, carry):
        encode(c, carry)
        chunk(c + RING).start()
        return carry

    lax.fori_loop(0, parts - RING, encode_more, 0)
    lax.fori_loop(parts - RING, parts, encode, 0)
    for copy in smalls:
        copy.wait()
    pl.semaphore_wait(barrier, devices - 1)

    def gather(read):
        def take(j, carry):
            found = [work[read(j, u)] for u in range(UNROLL)]
            for u in range(UNROLL):
                picked[j * UNROLL + u] = found[u]
            return carry

        lax.fori_loop(0, LANES // UNROLL, take, 0)
        return picked[...].reshape(LANES, width).astype(jnp.bfloat16)

    def peer(w, a):
        return turned(1 + ABREAST * (w // pieces) + a, n)

    def transfer(m, piece):
        at = m * pieces + piece
        return pltpu.make_async_remote_copy(
            src_ref=stage.at[at],
            dst_ref=recv.at[at],
            send_sem=send_sem.at[at],
            recv_sem=recv_sem.at[at],
            device_id=(dom, flipped(me, m, n)),
            device_id_type=MESH,
        )

    def pack_piece(m, piece):
        t = flipped(me, m, n)
        stage[m * pieces + piece] = gather(
            lambda j, u: packing[t, piece * LANES + j * UNROLL + u]
        )

    def pack(w, carry):
        for a in range(ABREAST):
            pack_piece(peer(w, a), w % pieces)
        return carry

    def start(w):
        for a in range(ABREAST):
            transfer(peer(w, a), w % pieces).start()

    def pack_start(w, carry):
        for a in range(ABREAST):
            pack_piece(peer(w, a), w % pieces)
            transfer(peer(w, a), w % pieces).start()
        return carry

    waves = (n - 1) // ABREAST * pieces
    alone = [turned(n - 1 - r, n) for r in range((n - 1) % ABREAST)]
    lax.fori_loop(0, AHEAD, pack_start, 0)
    for m in alone:

        def pack_alone(piece, carry):
            pack_piece(m, piece)
            transfer(m, piece).start()
            return carry

        lax.fori_loop(0, pieces, pack_alone, 0)
    for load in loads[1:]:
        load.start()

    def pack_own(piece, carry):
        pack_piece(0, piece)
        return carry

    lax.fori_loop(0, pieces, pack_own, 0)

    lane = lax.broadcasted_iota(jnp.int32, (LANES, LANES), 1)
    for c in range(rows // LANES):
        row = placing_row[0:1, c * LANES : (c + 1) * LANES]
        place_ids[c * LANES : (c + 1) * LANES, :] = (
            jnp.broadcast_to(row, (LANES, LANES)).T - lane
        )
    for c in range(rows // LANES):
        given = degree[c : c + 1, :].astype(jnp.float32)
        share[c * LANES : (c + 1) * LANES, :] = 1.0 / jnp.broadcast_to(given, (LANES, LANES)).T
    line_lane = lax.broadcasted_iota(jnp.int32, (1, LANES), 1)

    def edge_place(e, carry):
        for b in range(bound):
            row = sending_one[e, b]
            slot = placing[0, jnp.minimum(row, rows - 1)]
            slot = jnp.where(row < rows, slot, NOWHERE)
            edge_ids[pl.ds(e * bound + b, 1), :] = jnp.full((1, LANES), slot) - line_lane
        return carry

    lax.fori_loop(0, devices, edge_place, 0)
    zeros = jnp.zeros((size, width), jnp.bfloat16)
    owned[blocks] = zeros
    halo_mixed[far_blocks] = zeros

    def chosen(ids, firsts):
        return jnp.concatenate(
            [jnp.where(ids == first, 1.0, 0.0).astype(jnp.bfloat16) for first in firsts], axis=1
        )

    def place_edge(table, found_at, firsts, fresh):
        def body(r, carry):
            here = span(r * STEP, STEP)
            rhs = jnp.concatenate([table[at] for at in found_at], axis=0)
            found = dot(chosen(edge_ids[here, :], firsts), rhs).astype(jnp.bfloat16)
            edge[0, here, :] = found if fresh else edge[0, here, :] + found
            return carry

        lax.fori_loop(0, count // STEP, body, 0)

    def place(table, found_at, firsts, fresh):
        tall = 2 * STEP

        def body(r, carry):
            here = span(r * tall, tall)
            there = span(r * (tall // size), tall // size)
            rhs = jnp.concatenate([table[at] for at in found_at], axis=0)
            found = dot(chosen(place_ids[here, :], firsts), rhs)
            found = found.astype(jnp.bfloat16).reshape(tall // size, size, width)
            owned[there] = found if fresh else owned[there] + found
            return carry

        lax.fori_loop(0, rows // tall, body, 0)

    def whole_source(m):
        source = flipped(me, m, n) * cap
        return (
            [m * pieces + p for p in range(pieces)],
            [source + p * LANES for p in range(pieces)],
        )

    found_at, firsts = whole_source(0)
    place_edge(stage, found_at, firsts, True)
    place(stage, found_at, firsts, True)

    def wave(w):
        piece = w % pieces
        peers = [peer(w, a) for a in range(ABREAST)]
        return (
            [m * pieces + piece for m in peers],
            [flipped(me, m, n) * cap + piece * LANES for m in peers],
        )

    def arrive(w):
        for a in range(ABREAST):
            transfer(peer(w, a), w % pieces).wait()

    def take(first, total):
        found_at, firsts = [], []
        for w in range(first, first + total):
            at, source = wave(w)
            found_at, firsts = found_at + at, firsts + source
        place_edge(recv, found_at, firsts, False)
        place(recv, found_at, firsts, False)

    def gather_far(layer, index, live):
        def body(b, carry):
            for f in range(far_blocks):
                total = None
                for k in range(slots):
                    on = (k < live[b]) & (index[k, b] == blocks + f)
                    flag = jnp.where(on, 1.0, 0.0).astype(jnp.float32)
                    term = tiles[layer, b, k] * jnp.full((size, size), flag).astype(jnp.bfloat16)
                    total = term if total is None else total + term
                far_tiles[layer, span(b * size, size), f * size : (f + 1) * size] = total
            return carry

        lax.fori_loop(0, blocks, body, 0)

    paired = (waves - 2) // 2
    for p in range(paired):
        lax.fori_loop(min(2 * p + AHEAD, waves), min(2 * p + AHEAD + 2, waves), pack, 0)
        for w in (2 * p, 2 * p + 1):
            arrive(w)
            if w + AHEAD < waves:
                start(w + AHEAD)
        take(2 * p, 2)
        if p == 0:
            for m in alone:
                found_at, firsts = whole_source(m)

                def landed(piece, carry):
                    transfer(m, piece).wait()
                    return carry

                lax.fori_loop(0, pieces, landed, 0)
                place_edge(recv, found_at, firsts, False)
                place(recv, found_at, firsts, False)
        if p == 1:
            for load in loads[1:]:
                load.wait()
            if dense:
                gather_far(0, index_one, live_one)
                gather_far(1, index_two, live_two)
    for w in range(2 * paired, waves - 1):
        arrive(w)
        take(w, 1)

    def edge_start(layer):
        for away in [groups // 2] + [a for a in range(1, groups) if a != groups // 2] + [0]:
            to_dom = (dom + away) % groups
            for q in range(0 if away else 1, n):
                to_me = (me + q) % n
                pltpu.make_async_remote_copy(
                    src_ref=edge.at[layer, span((to_dom * n + to_me) * bound, bound), :],
                    dst_ref=halo.at[layer, span(flat * bound, bound), :],
                    send_sem=edge_send.at[layer],
                    recv_sem=edge_recv.at[layer],
                    device_id=(to_dom, to_me),
                    device_id_type=MESH,
                ).start()
        mine = span(flat * bound, bound)
        halo[layer, mine, :] = edge[layer, mine, :]

    def edge_wait(layer):
        most = pl.ds(0, count - bound)
        for sem in (edge_recv, edge_send):
            pltpu.make_async_copy(
                edge.at[layer, most, :], halo.at[layer, most, :], sem.at[layer]
            ).wait()

    arrive(waves - 1)
    found_at, firsts = wave(waves - 1)
    place_edge(recv, found_at, firsts, False)
    edge_start(0)
    place(recv, found_at, firsts, False)
    stage[blocks] = zeros
    work[rows] = jnp.zeros((wide, LANES), jnp.float32)

    def shared(layer, b, table, where):
        lhs = jnp.concatenate([tiles[layer, b, k] for k in range(slots)], axis=1)
        rhs = jnp.concatenate([table[where(b, k)] for k in range(slots)], axis=0)
        part = share[span(b * size, size), :]
        return dot(lhs, rhs) * jnp.concatenate([part] * wide, axis=1)

    def front(layer, source, index, live):
        def near(b, k):
            at = index[k, b]
            return jnp.where((k < live[b]) & (at < blocks), at, blocks)

        def body(step, carry):
            aggregate = jnp.concatenate(
                [
                    shared(layer, step * (2 * per_step) + j, source, near).astype(jnp.bfloat16)
                    for j in range((2 * per_step))
                ],
                axis=0,
            )
            own = source[span(step * (2 * per_step), (2 * per_step))].reshape(2 * STEP, width)
            mixed = dot(own, weights[2 * layer]) + dot(aggregate, weights[2 * layer + 1])
            work[span(step * 2 * STEP, 2 * STEP)] = mixed.reshape(2 * STEP, wide, LANES)
            return carry

        lax.fori_loop(0, parts // 2, body, 0)

    def project(layer):
        def mix(r, carry):
            mixed = dot(halo[layer, span(r * STEP, STEP), :], weights[2 * layer + 1])
            halo_mixed[span(r * per_step, per_step)] = mixed.astype(jnp.bfloat16).reshape(
                per_step, size, width
            )
            return carry

        lax.fori_loop(0, count // STEP, mix, 0)

    def back(layer, index, live, use):
        def far(b, k):
            at = index[k, b]
            return jnp.where((k < live[b]) & (at >= blocks), at - blocks, far_blocks)

        def body(step, carry):
            here = span(step * tall, tall)
            mixed = work[here].reshape(tall, width)
            if dense:
                table = halo_mixed[0:far_blocks].reshape(count, width)
                part = jnp.concatenate([share[here, :]] * wide, axis=1)
                mixed = mixed + dot(far_tiles[layer, here, :], table) * part
            else:
                mixed = mixed + jnp.concatenate(
                    [shared(layer, step * per_step + j, halo_mixed, far) for j in range(per_step)],
                    axis=0,
                )
            use(step, normal(mixed))
            return carry

        lax.fori_loop(0, rows // tall, body, 0)

    front(0, owned, index_one, live_one)
    edge_wait(0)

    def keep(step, result):
        stage[span(step * (tall // size), tall // size)] = result.reshape(-1, size, width)
        work[span(step * tall, tall)] = result.astype(jnp.float32).reshape(tall, wide, LANES)

    project(0)
    back(0, index_one, live_one, keep)

    def edge_pick(r, carry):
        def read(j, u):
            return sending_two[(r * LANES + j * UNROLL) // bound + u // bound, u % bound]

        edge[1, span(r * LANES, LANES), :] = gather(read)
        return carry

    lax.fori_loop(0, count // LANES, edge_pick, 0)
    edge_start(1)
    front(1, stage, index_two, live_two)
    edge_wait(1)
    project(1)
    if embedding is None:
        return

    heads = jnp.broadcast_to(head[...].astype(jnp.float32), (16, width)).astype(jnp.bfloat16)

    def finish(step, result):
        embedding[span(step * (tall // size), tall // size)] = result.reshape(-1, size, width)
        logits = lax.dot_general(
            heads, result, (((1,), (1,)), ((), ())), preferred_element_type=jnp.float32
        )
        probability[pl.ds(step, 1)] = jax.nn.sigmoid(logits[0:1, :])[None]

    back(1, index_two, live_two, finish)


def kernel_handing_on(groups, n, *refs):
    arguments, (work, far_tiles, halo_mixed, share), rest = refs[:19], refs[19:23], refs[23:]
    kernel(
        groups,
        n,
        *arguments,
        None,
        None,
        *rest[:4],
        work,
        *rest[4:10],
        share,
        *rest[10:12],
        halo_mixed,
        far_tiles,
        *rest[12:],
    )


def last_kernel(
    work, far_tiles, halo_mixed, share, head, embedding, probability, result, out_sem
):
    rows, width = result.shape
    wide = width // LANES
    count = far_tiles.shape[2]
    heads = jnp.broadcast_to(head[...].astype(jnp.float32), (16, width)).astype(jnp.bfloat16)
    table = halo_mixed.at[0 : halo_mixed.shape[0] - 1]

    def leaving(step):
        here = span(step * BACK, BACK)
        return pltpu.make_async_copy(result.at[here, :], embedding.at[here, :], out_sem.at[step])

    def body(step, carry):
        here = span(step * BACK, BACK)
        part = jnp.concatenate([share[here, :]] * wide, axis=1)
        far = dot(far_tiles[1, here, :], table[...].reshape(count, width))
        found = normal(work[here].reshape(BACK, width) + far * part)
        result[here, :] = found
        leaving(step).start()
        logits = lax.dot_general(
            heads, found, (((1,), (1,)), ((), ())), preferred_element_type=jnp.float32
        )
        probability[pl.ds(step, 1)] = jax.nn.sigmoid(logits[0:1, :])[None]
        return carry

    lax.fori_loop(0, rows // BACK, body, 0)

    def left(step, carry):
        leaving(step).wait()
        return carry

    lax.fori_loop(0, rows // BACK, left, 0)


def per_device(
    features,
    enc_weight,
    pack_index,
    place_index,
    halo_send_one,
    halo_send_two,
    tile_index_one,
    tile_index_two,
    tile_live_one,
    tile_live_two,
    tiles_one,
    tiles_two,
    degree,
    self_weight_one,
    neigh_weight_one,
    self_weight_two,
    neigh_weight_two,
    head_weight,
):
    groups, n = lax.axis_size("dom"), lax.axis_size("shard")
    rows, depth = features.shape
    width = enc_weight.shape[1]
    wide = width // LANES
    blocks, slots, size = tiles_one.shape[:3]
    bound = halo_send_one.shape[-1]
    devices = groups * n
    count = devices * bound
    cap = rows // n
    dense = count <= rows // 8
    tall = BACK if dense else STEP
    vmem = pl.BlockSpec(memory_space=pltpu.VMEM)
    hbm = pl.BlockSpec(memory_space=pl.ANY)
    bf16, f32, i32 = jnp.bfloat16, jnp.float32, jnp.int32
    handed = (
        pltpu.VMEM((rows + 2, wide, LANES), f32),
        pltpu.VMEM((2, rows, count), bf16),
        pltpu.VMEM((count // size + 1, size, width), bf16),
        pltpu.VMEM((rows, LANES), f32),
    )
    outputs = pl.pallas_call(
        functools.partial(kernel_handing_on if dense else kernel, groups, n),
        out_shape=handed
        if dense
        else (
            pltpu.VMEM((blocks, size, width), bf16),
            jax.ShapeDtypeStruct((rows // tall, 1, tall), f32),
        ),
        in_specs=[hbm] * 19,
        out_specs=(vmem,) * (len(handed) if dense else 2),
        scratch_shapes=[
            pltpu.VMEM((RING, STEP, depth), bf16),
            pltpu.VMEM((depth, width), bf16),
            pltpu.VMEM((4, width, width), bf16),
            pltpu.VMEM((2, blocks, slots, size, size), bf16),
        ]
        + ([] if dense else [handed[0]])
        + [
            pltpu.VMEM((LANES, wide, LANES), f32),
            pltpu.VMEM((blocks + 1, size, width), bf16),
            pltpu.VMEM((blocks, size, width), bf16),
            pltpu.VMEM((blocks + 1, size, width), bf16),
            pltpu.VMEM((rows, LANES), i32),
            pltpu.VMEM((count, LANES), i32),
        ]
        + ([] if dense else [handed[3]])
        + [pltpu.VMEM((2, count, width), bf16)] * 2
        + ([] if dense else [handed[2], pltpu.VMEM((2, size, count), bf16)])
        + [
            pltpu.SMEM((n, cap), i32),
            pltpu.SMEM((1, rows), i32),
            pltpu.VMEM((1, rows), i32),
            pltpu.SMEM((devices, bound), i32),
            pltpu.SMEM((devices, bound), i32),
            pltpu.SMEM((slots, blocks), i32),
            pltpu.SMEM((slots, blocks), i32),
            pltpu.SMEM((blocks,), i32),
            pltpu.SMEM((blocks,), i32),
            pltpu.VMEM((rows // LANES, LANES), i32),
            pltpu.VMEM((width,), bf16),
            pltpu.SemaphoreType.DMA((11,)),
            pltpu.SemaphoreType.DMA((RING,)),
            pltpu.SemaphoreType.DMA((7,)),
            pltpu.SemaphoreType.DMA((rows // LANES,)),
            pltpu.SemaphoreType.DMA((rows // LANES,)),
            pltpu.SemaphoreType.DMA((2,)),
            pltpu.SemaphoreType.DMA((2,)),
        ],
        compiler_params=pltpu.CompilerParams(
            collective_id=0,
            has_side_effects=True,
            vmem_limit_bytes=FIRST_LIMIT if dense else VMEM_LIMIT,
        ),
        cost_estimate=pl.CostEstimate(
            flops=2 * rows * width * (depth + rows + 4 * slots * size + 4 * width),
            bytes_accessed=rows * depth * 2 + tiles_one.size * 4 + rows * width * 2,
            transcendentals=0,
        ),
    )(
        features,
        enc_weight,
        tiles_one,
        tiles_two,
        self_weight_one,
        neigh_weight_one,
        self_weight_two,
        neigh_weight_two,
        pack_index.reshape(n, cap),
        place_index.reshape(1, rows),
        place_index.reshape(1, rows),
        halo_send_one.reshape(devices, bound),
        halo_send_two.reshape(devices, bound),
        tile_index_one.T,
        tile_index_two.T,
        tile_live_one,
        tile_live_two,
        degree.reshape(-1, LANES),
        head_weight,
    )
    if dense:
        outputs = pl.pallas_call(
            last_kernel,
            out_shape=(
                jax.ShapeDtypeStruct((rows, width), bf16),
                jax.ShapeDtypeStruct((rows // BACK, 1, BACK), f32),
            ),
            in_specs=[vmem] * 5,
            out_specs=(hbm, vmem),
            scratch_shapes=[
                pltpu.VMEM((rows, width), bf16),
                pltpu.SemaphoreType.DMA((rows // BACK,)),
            ],
            compiler_params=pltpu.CompilerParams(vmem_limit_bytes=LAST_LIMIT),
        )(*outputs, head_weight)
    embedding, probability = outputs
    return (embedding.reshape(rows, width), probability.reshape(-1))


def solution(mesh):
    placed = (
        P(("dom", "shard"), None),
        P(),
        P("dom", "shard", None, None),
        P("dom", "shard", None),
        P("dom", "shard", None, None, None),
        P("dom", "shard", None, None, None),
        P(("dom", "shard"), None),
        P(("dom", "shard"), None),
        P(("dom", "shard")),
        P(("dom", "shard")),
        P(("dom", "shard"), None, None, None),
        P(("dom", "shard"), None, None, None),
        P(("dom", "shard")),
        P(),
        P(),
        P(),
        P(),
        P(),
    )
    return jax.shard_map(
        per_device,
        mesh=mesh,
        in_specs=placed,
        out_specs=(P(("dom", "shard"), None), P(("dom", "shard"))),
        check_vma=False,
    )
```

```python
import functools

import jax
import jax.numpy as jnp
from jax import lax
from jax.experimental import pallas as pl
from jax.experimental.pallas import tpu as pltpu
from jax.sharding import PartitionSpec as P

LANES = 128
STEP = 512
RING = 4
UNROLL = 64
ABREAST = 3
AHEAD = 3
BACK = 1024
VMEM_LIMIT = 59 << 20
FIRST_LIMIT = 42 << 20
LAST_LIMIT = 16 << 20
MESH = pl.DeviceIdType.MESH
NOWHERE = -(1 << 20)


def dot(a, b):
    return jnp.dot(a, b, preferred_element_type=jnp.float32)


def span(first, count):
    return pl.ds(pl.multiple_of(first, count), count)


def flipped(a, b, n):
    total, bit = 0, 1
    while bit < n:
        p, q = (a // bit) % 2, (b // bit) % 2
        total = total + bit * (p + q - 2 * p * q)
        bit *= 2
    return total


def turned(step, n):
    half = n // 2
    return jnp.where(step < half, 2 * step, (2 * (step - half) + 3) % n)


def normal(mixed):
    active = jnp.maximum(mixed, 0.0)
    scale = lax.rsqrt(jnp.mean(active * active, axis=-1, keepdims=True) + 1e-06)
    return (active * scale).astype(jnp.bfloat16)


def kernel(
    groups,
    n,
    features,
    enc_weight,
    tiles_one,
    tiles_two,
    self_one,
    neigh_one,
    self_two,
    neigh_two,
    packing_in,
    placing_in,
    placing_row_in,
    sending_one_in,
    sending_two_in,
    index_one_in,
    index_two_in,
    live_one_in,
    live_two_in,
    degree_in,
    head_in,
    embedding,
    probability,
    feats,
    weight,
    weights,
    tiles,
    work,
    picked,
    stage,
    recv,
    owned,
    place_ids,
    edge_ids,
    share,
    edge,
    halo,
    halo_mixed,
    far_tiles,
    packing,
    placing,
    placing_row,
    sending_one,
    sending_two,
    index_one,
    index_two,
    live_one,
    live_two,
    degree,
    head,
    small_sem,
    feat_sem,
    load_sem,
    send_sem,
    recv_sem,
    edge_send,
    edge_recv,
):
    rows = features.shape[0]
    width = enc_weight.shape[1]
    wide = width // LANES
    cap = rows // n
    pieces = cap // LANES
    parts = rows // STEP
    devices = groups * n
    bound = sending_one.shape[1]
    count = devices * bound
    blocks, slots, size = tiles_one.shape[:3]
    per_step = STEP // size
    far_blocks = count // size
    dense = far_tiles.shape[1] == rows
    tall = BACK if dense else STEP
    dom, me = lax.axis_index("dom"), lax.axis_index("shard")
    flat = dom * n + me

    barrier = pltpu.get_barrier_semaphore()
    for away in range(groups):

        def greet(q, carry):
            to = ((dom + away) % groups, (me + q) % n)
            pl.semaphore_signal(barrier, inc=1, device_id=to, device_id_type=MESH)
            return carry

        lax.fori_loop(0 if away else 1, n, greet, 0)

    def chunk(c):
        return pltpu.make_async_copy(
            features.at[span(c * STEP, STEP), :], feats.at[c % RING], feat_sem.at[c % RING]
        )

    loads = [
        pltpu.make_async_copy(enc_weight, weight, load_sem.at[0]),
        pltpu.make_async_copy(tiles_one, tiles.at[0], load_sem.at[1]),
        pltpu.make_async_copy(tiles_two, tiles.at[1], load_sem.at[2]),
    ] + [
        pltpu.make_async_copy(source, weights.at[i], load_sem.at[3 + i])
        for i, source in enumerate((self_one, neigh_one, self_two, neigh_two))
    ]
    smalls = [
        pltpu.make_async_copy(source, target, small_sem.at[i])
        for i, (source, target) in enumerate(
            (
                (packing_in, packing),
                (placing_in, placing),
                (placing_row_in, placing_row),
                (sending_one_in, sending_one),
                (sending_two_in, sending_two),
                (index_one_in, index_one),
                (index_two_in, index_two),
                (live_one_in, live_one),
                (live_two_in, live_two),
                (degree_in, degree),
                (head_in, head),
            )
        )
    ]
    loads[0].start()
    for c in range(RING):
        chunk(c).start()
    for copy in smalls:
        copy.start()
    loads[0].wait()

    def encode(c, carry):
        chunk(c).wait()
        found = jnp.maximum(dot(feats[c % RING], weight[...]), 0.0)
        found = found.astype(jnp.bfloat16).astype(jnp.float32)
        work[span(c * STEP, STEP)] = found.reshape(STEP, wide, LANES)
        return carry

    def encode_more(c, carry):
        encode(c, carry)
        chunk(c + RING).start()
        return carry

    lax.fori_loop(0, parts - RING, encode_more, 0)
    lax.fori_loop(parts - RING, parts, encode, 0)
    for copy in smalls:
        copy.wait()

    def gather(read):
        def take(j, carry):
            found = [work[read(j, u)] for u in range(UNROLL)]
            for u in range(UNROLL):
                picked[j * UNROLL + u] = found[u]
            return carry

        lax.fori_loop(0, LANES // UNROLL, take, 0)
        return picked[...].reshape(LANES, width).astype(jnp.bfloat16)

    def peer(w, a):
        return turned(1 + ABREAST * (w // pieces) + a, n)

    def transfer(m, piece):
        at = m * pieces + piece
        return pltpu.make_async_remote_copy(
            src_ref=stage.at[at],
            dst_ref=recv.at[at],
            send_sem=send_sem.at[at],
            recv_sem=recv_sem.at[at],
            device_id=(dom, flipped(me, m, n)),
            device_id_type=MESH,
        )

    def pack_piece(m, piece):
        t = flipped(me, m, n)
        stage[m * pieces + piece] = gather(
            lambda j, u: packing[t, piece * LANES + j * UNROLL + u]
        )

    def pack(w, carry):
        for a in range(ABREAST):
            pack_piece(peer(w, a), w % pieces)
        return carry

    def start(w):
        for a in range(ABREAST):
            transfer(peer(w, a), w % pieces).start()

    def pack_start(w, carry):
        for a in range(ABREAST):
            pack_piece(peer(w, a), w % pieces)
            transfer(peer(w, a), w % pieces).start()
        return carry

    waves = (n - 1) // ABREAST * pieces
    alone = [turned(n - 1 - r, n) for r in range((n - 1) % ABREAST)]
    first = peer(0, 0)
    pack_piece(first, 0)
    pl.semaphore_wait(barrier, devices - 1)
    transfer(first, 0).start()
    for a in range(1, ABREAST):
        pack_piece(peer(0, a), 0)
        transfer(peer(0, a), 0).start()
    lax.fori_loop(1, AHEAD, pack_start, 0)
    for m in alone:

        def pack_alone(piece, carry):
            pack_piece(m, piece)
            transfer(m, piece).start()
            return carry

        lax.fori_loop(0, pieces, pack_alone, 0)
    for load in loads[1:]:
        load.start()

    def pack_own(piece, carry):
        pack_piece(0, piece)
        return carry

    lax.fori_loop(0, pieces, pack_own, 0)

    lane = lax.broadcasted_iota(jnp.int32, (LANES, LANES), 1)
    for c in range(rows // LANES):
        row = placing_row[0:1, c * LANES : (c + 1) * LANES]
        place_ids[c * LANES : (c + 1) * LANES, :] = (
            jnp.broadcast_to(row, (LANES, LANES)).T - lane
        )
    for c in range(rows // LANES):
        given = degree[c : c + 1, :].astype(jnp.float32)
        share[c * LANES : (c + 1) * LANES, :] = 1.0 / jnp.broadcast_to(given, (LANES, LANES)).T
    line_lane = lax.broadcasted_iota(jnp.int32, (1, LANES), 1)

    def edge_place(e, carry):
        for b in range(bound):
            row = sending_one[e, b]
            slot = placing[0, jnp.minimum(row, rows - 1)]
            slot = jnp.where(row < rows, slot, NOWHERE)
            edge_ids[pl.ds(e * bound + b, 1), :] = jnp.full((1, LANES), slot) - line_lane
        return carry

    lax.fori_loop(0, devices, edge_place, 0)
    zeros = jnp.zeros((size, width), jnp.bfloat16)
    owned[blocks] = zeros
    halo_mixed[far_blocks] = zeros

    def chosen(ids, firsts):
        return jnp.concatenate(
            [jnp.where(ids == first, 1.0, 0.0).astype(jnp.bfloat16) for first in firsts], axis=1
        )

    def place_edge(table, found_at, firsts, fresh):
        def body(r, carry):
            here = span(r * STEP, STEP)
            rhs = jnp.concatenate([table[at] for at in found_at], axis=0)
            found = dot(chosen(edge_ids[here, :], firsts), rhs).astype(jnp.bfloat16)
            edge[0, here, :] = found if fresh else edge[0, here, :] + found
            return carry

        lax.fori_loop(0, count // STEP, body, 0)

    def place(table, found_at, firsts, fresh):
        tall = 2 * STEP

        def body(r, carry):
            here = span(r * tall, tall)
            there = span(r * (tall // size), tall // size)
            rhs = jnp.concatenate([table[at] for at in found_at], axis=0)
            found = dot(chosen(place_ids[here, :], firsts), rhs)
            found = found.astype(jnp.bfloat16).reshape(tall // size, size, width)
            owned[there] = found if fresh else owned[there] + found
            return carry

        lax.fori_loop(0, rows // tall, body, 0)

    def whole_source(m):
        source = flipped(me, m, n) * cap
        return (
            [m * pieces + p for p in range(pieces)],
            [source + p * LANES for p in range(pieces)],
        )

    found_at, firsts = whole_source(0)
    place_edge(stage, found_at, firsts, True)
    place(stage, found_at, firsts, True)

    def wave(w):
        piece = w % pieces
        peers = [peer(w, a) for a in range(ABREAST)]
        return (
            [m * pieces + piece for m in peers],
            [flipped(me, m, n) * cap + piece * LANES for m in peers],
        )

    def arrive(w):
        for a in range(ABREAST):
            transfer(peer(w, a), w % pieces).wait()

    def take(first, total):
        found_at, firsts = [], []
        for w in range(first, first + total):
            at, source = wave(w)
            found_at, firsts = found_at + at, firsts + source
        place_edge(recv, found_at, firsts, False)
        place(recv, found_at, firsts, False)

    def gather_far(layer, index, live):
        def body(b, carry):
            for f in range(far_blocks):
                total = None
                for k in range(slots):
                    on = (k < live[b]) & (index[k, b] == blocks + f)
                    flag = jnp.where(on, 1.0, 0.0).astype(jnp.float32)
                    term = tiles[layer, b, k] * jnp.full((size, size), flag).astype(jnp.bfloat16)
                    total = term if total is None else total + term
                far_tiles[layer, span(b * size, size), f * size : (f + 1) * size] = total
            return carry

        lax.fori_loop(0, blocks, body, 0)

    paired = (waves - 2) // 2
    for p in range(paired):
        lax.fori_loop(min(2 * p + AHEAD, waves), min(2 * p + AHEAD + 2, waves), pack, 0)
        for w in (2 * p, 2 * p + 1):
            arrive(w)
            if w + AHEAD < waves:
                start(w + AHEAD)
        take(2 * p, 2)
        if p == 0:
            for m in alone:
                found_at, firsts = whole_source(m)

                def landed(piece, carry):
                    transfer(m, piece).wait()
                    return carry

                lax.fori_loop(0, pieces, landed, 0)
                place_edge(recv, found_at, firsts, False)
                place(recv, found_at, firsts, False)
        if p == 1:
            for load in loads[1:]:
                load.wait()
            if dense:
                gather_far(0, index_one, live_one)
                gather_far(1, index_two, live_two)
    for w in range(2 * paired, waves - 1):
        arrive(w)
        take(w, 1)

    def edge_start(layer):
        for away in [groups // 2] + [a for a in range(1, groups) if a != groups // 2] + [0]:
            to_dom = (dom + away) % groups
            for q in range(0 if away else 1, n):
                to_me = (me + q) % n
                pltpu.make_async_remote_copy(
                    src_ref=edge.at[layer, span((to_dom * n + to_me) * bound, bound), :],
                    dst_ref=halo.at[layer, span(flat * bound, bound), :],
                    send_sem=edge_send.at[layer],
                    recv_sem=edge_recv.at[layer],
                    device_id=(to_dom, to_me),
                    device_id_type=MESH,
                ).start()
        mine = span(flat * bound, bound)
        halo[layer, mine, :] = edge[layer, mine, :]

    def edge_wait(layer):
        most = pl.ds(0, count - bound)
        for sem in (edge_recv, edge_send):
            pltpu.make_async_copy(
                edge.at[layer, most, :], halo.at[layer, most, :], sem.at[layer]
            ).wait()

    arrive(waves - 1)
    found_at, firsts = wave(waves - 1)
    place_edge(recv, found_at, firsts, False)
    edge_start(0)
    place(recv, found_at, firsts, False)
    stage[blocks] = zeros
    work[rows] = jnp.zeros((wide, LANES), jnp.float32)

    def shared(layer, b, table, where):
        lhs = jnp.concatenate([tiles[layer, b, k] for k in range(slots)], axis=1)
        rhs = jnp.concatenate([table[where(b, k)] for k in range(slots)], axis=0)
        part = share[span(b * size, size), :]
        return dot(lhs, rhs) * jnp.concatenate([part] * wide, axis=1)

    def front(layer, source, index, live):
        def near(b, k):
            at = index[k, b]
            return jnp.where((k < live[b]) & (at < blocks), at, blocks)

        def body(step, carry):
            aggregate = jnp.concatenate(
                [
                    shared(layer, step * (2 * per_step) + j, source, near).astype(jnp.bfloat16)
                    for j in range((2 * per_step))
                ],
                axis=0,
            )
            own = source[span(step * (2 * per_step), (2 * per_step))].reshape(2 * STEP, width)
            mixed = dot(own, weights[2 * layer]) + dot(aggregate, weights[2 * layer + 1])
            work[span(step * 2 * STEP, 2 * STEP)] = mixed.reshape(2 * STEP, wide, LANES)
            return carry

        lax.fori_loop(0, parts // 2, body, 0)

    def project(layer):
        def mix(r, carry):
            mixed = dot(halo[layer, span(r * STEP, STEP), :], weights[2 * layer + 1])
            halo_mixed[span(r * per_step, per_step)] = mixed.astype(jnp.bfloat16).reshape(
                per_step, size, width
            )
            return carry

        lax.fori_loop(0, count // STEP, mix, 0)

    def back(layer, index, live, use):
        def far(b, k):
            at = index[k, b]
            return jnp.where((k < live[b]) & (at >= blocks), at - blocks, far_blocks)

        def body(step, carry):
            here = span(step * tall, tall)
            mixed = work[here].reshape(tall, width)
            if dense:
                table = halo_mixed[0:far_blocks].reshape(count, width)
                part = jnp.concatenate([share[here, :]] * wide, axis=1)
                mixed = mixed + dot(far_tiles[layer, here, :], table) * part
            else:
                mixed = mixed + jnp.concatenate(
                    [shared(layer, step * per_step + j, halo_mixed, far) for j in range(per_step)],
                    axis=0,
                )
            use(step, normal(mixed))
            return carry

        lax.fori_loop(0, rows // tall, body, 0)

    front(0, owned, index_one, live_one)
    edge_wait(0)

    def keep(step, result):
        stage[span(step * (tall // size), tall // size)] = result.reshape(-1, size, width)
        work[span(step * tall, tall)] = result.astype(jnp.float32).reshape(tall, wide, LANES)

    project(0)
    back(0, index_one, live_one, keep)

    def edge_pick(r, carry):
        def read(j, u):
            return sending_two[(r * LANES + j * UNROLL) // bound + u // bound, u % bound]

        edge[1, span(r * LANES, LANES), :] = gather(read)
        return carry

    lax.fori_loop(0, count // LANES, edge_pick, 0)
    edge_start(1)
    front(1, stage, index_two, live_two)
    edge_wait(1)
    project(1)
    if embedding is None:
        return

    heads = jnp.broadcast_to(head[...].astype(jnp.float32), (16, width)).astype(jnp.bfloat16)

    def finish(step, result):
        embedding[span(step * (tall // size), tall // size)] = result.reshape(-1, size, width)
        logits = lax.dot_general(
            heads, result, (((1,), (1,)), ((), ())), preferred_element_type=jnp.float32
        )
        probability[pl.ds(step, 1)] = jax.nn.sigmoid(logits[0:1, :])[None]

    back(1, index_two, live_two, finish)


def kernel_handing_on(groups, n, *refs):
    arguments, (work, far_tiles, halo_mixed, share), rest = refs[:19], refs[19:23], refs[23:]
    kernel(
        groups,
        n,
        *arguments,
        None,
        None,
        *rest[:4],
        work,
        *rest[4:10],
        share,
        *rest[10:12],
        halo_mixed,
        far_tiles,
        *rest[12:],
    )


def last_kernel(
    work, far_tiles, halo_mixed, share, head, embedding, probability, result, out_sem
):
    rows, width = result.shape
    wide = width // LANES
    count = far_tiles.shape[2]
    heads = jnp.broadcast_to(head[...].astype(jnp.float32), (16, width)).astype(jnp.bfloat16)
    table = halo_mixed.at[0 : halo_mixed.shape[0] - 1]

    def leaving(step):
        here = span(step * BACK, BACK)
        return pltpu.make_async_copy(result.at[here, :], embedding.at[here, :], out_sem.at[step])

    def body(step, carry):
        here = span(step * BACK, BACK)
        part = jnp.concatenate([share[here, :]] * wide, axis=1)
        far = dot(far_tiles[1, here, :], table[...].reshape(count, width))
        found = normal(work[here].reshape(BACK, width) + far * part)
        result[here, :] = found
        leaving(step).start()
        logits = lax.dot_general(
            heads, found, (((1,), (1,)), ((), ())), preferred_element_type=jnp.float32
        )
        probability[pl.ds(step, 1)] = jax.nn.sigmoid(logits[0:1, :])[None]
        return carry

    lax.fori_loop(0, rows // BACK, body, 0)

    def left(step, carry):
        leaving(step).wait()
        return carry

    lax.fori_loop(0, rows // BACK, left, 0)


def per_device(
    features,
    enc_weight,
    pack_index,
    place_index,
    halo_send_one,
    halo_send_two,
    tile_index_one,
    tile_index_two,
    tile_live_one,
    tile_live_two,
    tiles_one,
    tiles_two,
    degree,
    self_weight_one,
    neigh_weight_one,
    self_weight_two,
    neigh_weight_two,
    head_weight,
):
    groups, n = lax.axis_size("dom"), lax.axis_size("shard")
    rows, depth = features.shape
    width = enc_weight.shape[1]
    wide = width // LANES
    blocks, slots, size = tiles_one.shape[:3]
    bound = halo_send_one.shape[-1]
    devices = groups * n
    count = devices * bound
    cap = rows // n
    dense = count <= rows // 8
    tall = BACK if dense else STEP
    vmem = pl.BlockSpec(memory_space=pltpu.VMEM)
    hbm = pl.BlockSpec(memory_space=pl.ANY)
    bf16, f32, i32 = jnp.bfloat16, jnp.float32, jnp.int32
    handed = (
        pltpu.VMEM((rows + 2, wide, LANES), f32),
        pltpu.VMEM((2, rows, count), bf16),
        pltpu.VMEM((count // size + 1, size, width), bf16),
        pltpu.VMEM((rows, LANES), f32),
    )
    outputs = pl.pallas_call(
        functools.partial(kernel_handing_on if dense else kernel, groups, n),
        out_shape=handed
        if dense
        else (
            pltpu.VMEM((blocks, size, width), bf16),
            jax.ShapeDtypeStruct((rows // tall, 1, tall), f32),
        ),
        in_specs=[hbm] * 19,
        out_specs=(vmem,) * (len(handed) if dense else 2),
        scratch_shapes=[
            pltpu.VMEM((RING, STEP, depth), bf16),
            pltpu.VMEM((depth, width), bf16),
            pltpu.VMEM((4, width, width), bf16),
            pltpu.VMEM((2, blocks, slots, size, size), bf16),
        ]
        + ([] if dense else [handed[0]])
        + [
            pltpu.VMEM((LANES, wide, LANES), f32),
            pltpu.VMEM((blocks + 1, size, width), bf16),
            pltpu.VMEM((blocks, size, width), bf16),
            pltpu.VMEM((blocks + 1, size, width), bf16),
            pltpu.VMEM((rows, LANES), i32),
            pltpu.VMEM((count, LANES), i32),
        ]
        + ([] if dense else [handed[3]])
        + [pltpu.VMEM((2, count, width), bf16)] * 2
        + ([] if dense else [handed[2], pltpu.VMEM((2, size, count), bf16)])
        + [
            pltpu.SMEM((n, cap), i32),
            pltpu.SMEM((1, rows), i32),
            pltpu.VMEM((1, rows), i32),
            pltpu.SMEM((devices, bound), i32),
            pltpu.SMEM((devices, bound), i32),
            pltpu.SMEM((slots, blocks), i32),
            pltpu.SMEM((slots, blocks), i32),
            pltpu.SMEM((blocks,), i32),
            pltpu.SMEM((blocks,), i32),
            pltpu.VMEM((rows // LANES, LANES), i32),
            pltpu.VMEM((width,), bf16),
            pltpu.SemaphoreType.DMA((11,)),
            pltpu.SemaphoreType.DMA((RING,)),
            pltpu.SemaphoreType.DMA((7,)),
            pltpu.SemaphoreType.DMA((rows // LANES,)),
            pltpu.SemaphoreType.DMA((rows // LANES,)),
            pltpu.SemaphoreType.DMA((2,)),
            pltpu.SemaphoreType.DMA((2,)),
        ],
        compiler_params=pltpu.CompilerParams(
            collective_id=0,
            has_side_effects=True,
            vmem_limit_bytes=FIRST_LIMIT if dense else VMEM_LIMIT,
        ),
        cost_estimate=pl.CostEstimate(
            flops=2 * rows * width * (depth + rows + 4 * slots * size + 4 * width),
            bytes_accessed=rows * depth * 2 + tiles_one.size * 4 + rows * width * 2,
            transcendentals=0,
        ),
    )(
        features,
        enc_weight,
        tiles_one,
        tiles_two,
        self_weight_one,
        neigh_weight_one,
        self_weight_two,
        neigh_weight_two,
        pack_index.reshape(n, cap),
        place_index.reshape(1, rows),
        place_index.reshape(1, rows),
        halo_send_one.reshape(devices, bound),
        halo_send_two.reshape(devices, bound),
        tile_index_one.T,
        tile_index_two.T,
        tile_live_one,
        tile_live_two,
        degree.reshape(-1, LANES),
        head_weight,
    )
    if dense:
        outputs = pl.pallas_call(
            last_kernel,
            out_shape=(
                jax.ShapeDtypeStruct((rows, width), bf16),
                jax.ShapeDtypeStruct((rows // BACK, 1, BACK), f32),
            ),
            in_specs=[vmem] * 5,
            out_specs=(hbm, vmem),
            scratch_shapes=[
                pltpu.VMEM((rows, width), bf16),
                pltpu.SemaphoreType.DMA((rows // BACK,)),
            ],
            compiler_params=pltpu.CompilerParams(vmem_limit_bytes=LAST_LIMIT),
        )(*outputs, head_weight)
    embedding, probability = outputs
    return (embedding.reshape(rows, width), probability.reshape(-1))


def solution(mesh):
    placed = (
        P(("dom", "shard"), None),
        P(),
        P("dom", "shard", None, None),
        P("dom", "shard", None),
        P("dom", "shard", None, None, None),
        P("dom", "shard", None, None, None),
        P(("dom", "shard"), None),
        P(("dom", "shard"), None),
        P(("dom", "shard")),
        P(("dom", "shard")),
        P(("dom", "shard"), None, None, None),
        P(("dom", "shard"), None, None, None),
        P(("dom", "shard")),
        P(),
        P(),
        P(),
        P(),
        P(),
    )
    return jax.shard_map(
        per_device,
        mesh=mesh,
        in_specs=placed,
        out_specs=(P(("dom", "shard"), None), P(("dom", "shard"))),
        check_vma=False,
    )
```
